1024 devices in a mesh: orb: 64 (over y, x, core), grid: 16 (over z).
Axes of the slice: x: 4, y: 8, z: 16, core: 2. Of those that a mesh axis runs over, the one named last changes fastest.
Arguments:
- wavefunctions: float32 [512, 96, 1024], P('orb', 'grid'), may hold values from -2 to 2
- potential: float32 [96, 1024], P('grid'), may hold values from -3 to 0
Outputs:
- orbitals: float32 [512, 96, 1024], P('orb', 'grid')
The draws below stay inside these ranges and needn't reach their ends.
All inputs are finite; a program needn't handle non-finite values.
Results may differ from the reference program's by a relative error of at most 0.0003.
Values sent between devices are 32-bit elements; how exact they have to be, the bound alone decides.
A program may use at most 32 MiB of HBM per device.

```python
import jax
import jax.numpy as jnp
from jax import lax

PANEL = 32
NPANEL = 2
NX = 32
NY = 32
NZ = 96
ORBS = 512


def block_levels(stream_key, extent, shards, least, high):
    factor_of, own = 1.0, jax.random.fold_in(stream_key, 6)
    for dim, parts in shards:
        steps = jnp.exp(jax.random.uniform(jax.random.fold_in(own, dim), (parts,), jnp.float32, least / len(shards), high / len(shards)))
        factor_of = factor_of * jnp.repeat(steps, extent[dim] // parts).reshape([-1 if axis == dim else 1 for axis in range(len(extent))])
    return factor_of


def centred(key, dims, width, reach, cuts=(), kind=jnp.bfloat16):
    drawn = jax.random.normal(key, dims, jnp.float32) * width
    if len(cuts) > 0:
        drawn = block_levels(key, dims, cuts, -0.22, 0.18) * drawn
    return jnp.clip(drawn, min=-reach, max=reach).astype(kind)


def setup_inputs(seed: int = 0) -> dict:
    splits = jax.random.split(jax.random.key(seed), 3)
    return {
        "wavefunctions": centred(splits[0], (ORBS, NZ, NX * NY), 0.25, 2.0, ((0, 64), (1, 16)), jnp.float32),
        "potential": jnp.clip(-3.0 + 3.0 * jax.random.uniform(splits[1], (NZ, NX * NY), jnp.float32) ** block_levels(splits[1], (NZ, NX * NY), ((0, 16),), -0.2, 0.2), -3.0, 0.0),
    }


COEFFS = (-5369.0 / 1800.0, 12.0 / 7.0, -15.0 / 56.0, 10.0 / 189.0, -1.0 / 112.0, 2.0 / 1925.0, -1.0 / 16632.0)
HIGH = lax.Precision.HIGHEST

def hamiltonian(args):
    block, potential = args
    count = block.shape[0]
    grid = block.reshape(count, NZ, NX, NY)
    padded = jnp.pad(grid, ((0, 0), (0, 0), (6, 6), (6, 6)))
    total = 3.0 * COEFFS[0] * grid
    for k in range(1, 7):
        total = total + COEFFS[k] * (jnp.roll(grid, -k, 1) + jnp.roll(grid, k, 1) + padded[:, :, 6 + k:6 + k + NX, 6:6 + NY] + padded[:, :, 6 - k:6 - k + NX, 6:6 + NY] + padded[:, :, 6:6 + NX, 6 + k:6 + k + NY] + padded[:, :, 6:6 + NX, 6 - k:6 - k + NY])
    result = -0.5 * total.reshape(count, NZ * NX * NY) + (potential[None] * block).reshape(count, NZ * NX * NY)
    return result

def reference(wavefunctions, potential):
    scale = 1.0 / (NZ * NX * NY)
    nblocks = ORBS // PANEL
    blocks = wavefunctions.reshape(nblocks, PANEL, NZ, NX * NY)
    blocks = lax.map(lambda blk: hamiltonian((blk, potential)), blocks)
    for p in range(NPANEL):
        current = blocks[p]
        gram = jnp.einsum('ic,jc->ij', current, current, precision=HIGH) * scale
        lower = jnp.linalg.cholesky(gram)
        ortho = lax.linalg.triangular_solve(lower, current, left_side=True, lower=True)

        def project(args):
            blk, index = args
            coeff = jnp.einsum('ic,jc->ij', ortho, blk, precision=HIGH) * scale
            moved = blk - jnp.einsum('ij,ic->jc', coeff, ortho, precision=HIGH)
            return jnp.where(index > p, moved, jnp.where(index == p, ortho, blk))
        blocks = lax.map(project, (blocks, jnp.arange(nblocks, dtype=jnp.int32)))
    return blocks.reshape(ORBS, NZ, NX * NY)
```

```python
import functools

import jax
import jax.numpy as jnp
from jax import lax
from jax.experimental import pallas as pl
from jax.experimental.pallas import tpu as pltpu
from jax.sharding import PartitionSpec as P

PANEL = 32
NPANEL = 2
NY = 32
NXC = 4
ROWS = PANEL * NPANEL

COEFFS = (
    -5369.0 / 1800.0,
    12.0 / 7.0,
    -15.0 / 56.0,
    10.0 / 189.0,
    -1.0 / 112.0,
    2.0 / 1925.0,
    -1.0 / 16632.0,
)
RIM = 6
MESH = pl.DeviceIdType.MESH
F32 = jnp.float32
BF16 = jnp.bfloat16


def split(value):
    high = value.astype(BF16)
    return high, (value - high.astype(F32)).astype(BF16)


def nt(left, right):
    return lax.dot_general(left, right, (((1,), (1,)), ((), ())), preferred_element_type=F32)


def in_plane(v, v0_term):
    width = v.shape[1]
    lane = lax.broadcasted_iota(jnp.int32, v.shape, 1)
    column = lane % NY
    total = v0_term
    for k in range(1, RIM + 1):
        far = k * NY
        part = jnp.where(lane < width - far, pltpu.roll(v, width - far, 1), 0.0)
        part += jnp.where(lane >= far, pltpu.roll(v, far, 1), 0.0)
        part += jnp.where(column < NY - k, pltpu.roll(v, width - k, 1), 0.0)
        part += jnp.where(column >= k, pltpu.roll(v, k, 1), 0.0)
        total += (-0.5 * COEFFS[k]) * part
    return total


def order_of(depth):
    return sorted(range(depth), key=lambda p: (max(depth - p, p + 1), p))


def gather_kernel(
    scale, v_ref, pot_ref, work_ref, pieces_ref, gram_ref, coef_ref,
    own, halo, panel, part, zbuf, rest,
    hsend, hrecv, asend, arecv, zsend, zrecv, gsend, grecv,
):
    count, depth, plane = v_ref.shape
    nz, norb = lax.axis_size("grid"), lax.axis_size("orb")
    ny = norb // (2 * NXC)
    z, o = lax.axis_index("grid"), lax.axis_index("orb")
    y, x, c = o // (2 * NXC), (o // 2) % NXC, o % 2

    def at(yy, xx, cc):
        return (yy * NXC + xx) * 2 + cc

    partner = at(y, x, 1 - c)
    right, left = at(y, (x + 1) % NXC, c), at(y, (x + NXC - 1) % NXC, c)
    y_up, y_down = at((y + 1) % ny, x, c), at((y + ny - 1) % ny, x, c)
    order = order_of(depth)

    barrier = pltpu.get_barrier_semaphore()

    def greet_z(d, carry):
        pl.semaphore_signal(barrier, inc=1, device_id=(o, (z + d) % nz), device_id_type=MESH)
        return carry

    def greet_y(d, carry):
        pl.semaphore_signal(barrier, inc=1, device_id=(at((y + d) % ny, x, c), z), device_id_type=MESH)
        return carry

    lax.fori_loop(1, nz, greet_z, 0)
    lax.fori_loop(1, ny, greet_y, 0)
    for peer in (partner, right, left):
        pl.semaphore_signal(barrier, inc=1, device_id=(peer, z), device_id_type=MESH)

    for p in range(depth):
        own[p] = v_ref[:, p, :]

    pl.semaphore_wait(barrier, (nz - 1) + (ny - 1) + 3)

    halo_copies = []
    for i in range(depth):
        for side, p, peer in ((0, depth - 1 - i, (z + 1) % nz), (1, i, (z + nz - 1) % nz)):
            copy = pltpu.make_async_remote_copy(
                src_ref=own.at[p],
                dst_ref=halo.at[side, p],
                send_sem=hsend.at[side, p],
                recv_sem=hrecv.at[side, p],
                device_id=(o, peer),
                device_id_type=MESH,
            )
            copy.start()
            halo_copies.append(copy)
    arrived = {(0, depth - 1 - i // 2) if i % 2 == 0 else (1, i // 2): copy for i, copy in enumerate(halo_copies)}

    def flat(p, carry):
        v = own[p]
        rest[p] = in_plane(v, (pot_ref[pl.ds(p, 1), :] - 1.5 * COEFFS[0]) * v)
        return carry

    lax.fori_loop(0, depth, flat, 0)

    def slab(xx, cc):
        return (xx % NXC) * 2 + cc

    mine = slab(x, c)

    def copy_of(kind, s, p, peer):
        rows = pl.ds(pl.multiple_of(s * count, count), count)
        return pltpu.make_async_remote_copy(
            src_ref=panel.at[p, rows, :],
            dst_ref=panel.at[p, rows, :],
            send_sem=asend.at[kind, p],
            recv_sem=arecv.at[s, p],
            device_id=(peer, z),
            device_id_type=MESH,
        )

    goes_up = y <= ny // 2 - 1
    goes_down = (y == 0) | (y >= ny // 2 + 2)

    seen = set()
    for p in order:
        need = [(0, q) for q in range(p, depth)] + [(1, q) for q in range(0, p + 1)]
        for key in need:
            if key not in seen:
                seen.add(key)
                arrived[key].wait_recv()
        total = rest[p]
        for k in range(1, RIM + 1):
            after = own[p + k] if p + k < depth else halo[1, p + k - depth]
            before = own[p - k] if p - k >= 0 else halo[0, p - k + depth]
            total += (-0.5 * COEFFS[k]) * (after + before)
        work_ref[p] = total

        @pl.when(y == 0)
        def _():
            panel[p, pl.ds(pl.multiple_of(mine * count, count), count), :] = total
            copy_of(0, mine, p, y_up).start()
            copy_of(1, mine, p, y_down).start()
            copy_of(2, mine, p, right).start()
            copy_of(3, mine, p, left).start()
            copy_of(5, mine, p, partner).start()

    lag_near, lag_far = 2, 4
    half = depth // 2
    for t in range(depth + lag_far):
        if t < depth:
            p = order[t]

            @pl.when(y != 0)
            def _():
                copy_of(0, mine, p, y_up).wait_recv()
                copy_of(2, mine, p, right).start()
                copy_of(3, mine, p, left).start()
                copy_of(5, mine, p, partner).start()

                @pl.when(goes_up)
                def _():
                    copy_of(0, mine, p, y_up).start()

                @pl.when(goes_down)
                def _():
                    copy_of(1, mine, p, y_down).start()

        i = t - lag_near
        if 0 <= i < depth:
            p = order[i]
            from_left, from_right = slab(x + NXC - 1, c), slab(x + 1, c)
            copy_of(2, from_left, p, right).wait_recv()
            if i % 2 == 0:
                copy_of(4, from_left, p, right).start()
            copy_of(6, from_left, p, partner).start()
            copy_of(3, from_right, p, left).wait_recv()
            if i % 2 == 1:
                copy_of(4, from_right, p, left).start()
            copy_of(7, from_right, p, partner).start()
        i = t - lag_far
        if 0 <= i < depth:
            p = order[i]
            far = slab(x + 2, c)
            copy_of(4, far, p, right).wait_recv()
            copy_of(8, far, p, partner).start()

    part[...] = jnp.zeros_like(part)
    for p in order:
        for xx in range(NXC):
            copy_of(5, slab(xx, 1 - c), p, partner).wait_recv()
        high, low = split(panel[p])
        pieces = jnp.concatenate([high, low], axis=0)
        pieces_ref[p] = pieces

        @pl.when(y == 0)
        def _():
            product = nt(pieces, pieces)
            part[...] += product[:ROWS] + product[ROWS:]

        @pl.when(y != 0)
        def _():
            own_high, own_low = split(work_ref[p])
            product = nt(jnp.concatenate([own_high, own_low], axis=0), pieces)
            part[0:count] += product[:count] + product[count:]

    half_rows = ROWS // 2

    @pl.when(y == 0)
    def _():
        both = part[...]
        both = (both + pltpu.roll(both, ROWS, 1)) * scale
        lane = lax.broadcasted_iota(jnp.int32, (half_rows, 2 * ROWS), 1)
        zbuf[z] = jnp.where(lane < ROWS, both[:half_rows], both[half_rows:])

    @pl.when(y != 0)
    def _():
        both = part[0:count]
        zbuf[z, 0:count] = (both + pltpu.roll(both, ROWS, 1)) * scale

    def z_copy(origin, to, slot, rows):
        return pltpu.make_async_remote_copy(
            src_ref=zbuf.at[origin, pl.ds(0, rows), :],
            dst_ref=zbuf.at[origin, pl.ds(0, rows), :],
            send_sem=zsend.at[slot],
            recv_sem=zrecv.at[origin],
            device_id=(o, to),
            device_id_type=MESH,
        )

    def exchange(rows):
        def send(d, carry):
            z_copy(z, (z + d) % nz, d, rows).start()
            return carry

        def take(d, carry):
            z_copy((z + d) % nz, z, 0, rows).wait_recv()
            return carry

        def sent(d, carry):
            z_copy(z, (z + d) % nz, d, rows).wait_send()
            return carry

        lax.fori_loop(1, nz, send, 0)
        lax.fori_loop(1, nz, take, 0)
        total = zbuf[0, 0:rows]
        for i in range(1, 16):
            total += zbuf[i, 0:rows]
        lax.fori_loop(1, nz, sent, 0)
        return total

    def g_copy(d):
        return pltpu.make_async_remote_copy(
            src_ref=gram_ref,
            dst_ref=gram_ref,
            send_sem=gsend.at[d],
            recv_sem=grecv,
            device_id=(at((y + d) % ny, x, c), z),
            device_id_type=MESH,
        )

    @pl.when(y == 0)
    def _():
        gram_ref[...] = exchange(half_rows)
        coef_ref[...] = jnp.zeros_like(coef_ref)
        for d in range(1, 8):
            g_copy(d).start()
        for d in range(1, 8):
            g_copy(d).wait_send()

    @pl.when(y != 0)
    def _():
        coef_ref[...] = exchange(count)
        g_copy(1).wait_recv()

    for copy in halo_copies:
        copy.wait_send()
    for p in range(depth):

        @pl.when(goes_up)
        def _():
            copy_of(0, mine, p, y_up).wait_send()

        @pl.when(goes_down)
        def _():
            copy_of(1, mine, p, y_down).wait_send()

        for kind in range(2, 9):
            copy_of(kind, mine, p, partner).wait_send()


def correct_kernel(work_ref, pieces_ref, gram_ref, coef_ref, out_ref, inverse):
    count, depth, plane = out_ref.shape
    o = lax.axis_index("orb")
    half_rows = ROWS // 2
    packed = gram_ref[...]
    row = lax.broadcasted_iota(jnp.int32, (ROWS, 2 * ROWS), 0)
    lane = lax.broadcasted_iota(jnp.int32, (ROWS, 2 * ROWS), 1)
    full = jnp.concatenate([packed, pltpu.roll(packed, ROWS, 1)], axis=0)
    matrix = jnp.where(lane < ROWS, full, jnp.where(lane - ROWS == row, 1.0, 0.0))
    for k in range(ROWS - 1):
        base = (k // 8) * 8
        pivot_row = matrix[k : k + 1, :]
        scaled = pivot_row / matrix[k : k + 1, k : k + 1]
        below = matrix[base:, :]
        column = below[:, k : k + 1]
        below_row = row[base:, 0:1]
        column = jnp.where(below_row > k, column, 0.0)
        below = below - column * scaled
        matrix = below if base == 0 else jnp.concatenate([matrix[:base], below], axis=0)
    diagonal = jnp.sum(jnp.where(lane == row, matrix, 0.0), axis=1, keepdims=True)
    inverse[...] = matrix * lax.rsqrt(diagonal)

    lower_inverse = pltpu.roll(inverse[...], ROWS, 1)[:, :ROWS]
    coef = coef_ref[:, :ROWS]
    high = lax.Precision.HIGHEST
    solved = lax.dot_general(coef, lower_inverse, (((1,), (1,)), ((), ())), precision=high, preferred_element_type=F32)
    factor = -lax.dot_general(solved, lower_inverse, (((1,), (0,)), ((), ())), precision=high, preferred_element_type=F32)
    in_panel = o * count < ROWS
    start = pl.multiple_of(jnp.minimum(o * count, ROWS - count), count)
    rows = pltpu.roll(inverse[pl.ds(start, count), :], ROWS, 1)[:, :ROWS]
    factor = jnp.where(in_panel, rows, factor)
    keep = jnp.where(in_panel, 0.0, 1.0)
    f_high, f_low = split(factor)
    both = jnp.concatenate([jnp.concatenate([f_high, f_high], axis=1), jnp.concatenate([f_low, f_low], axis=1)], axis=0)
    for p in range(depth):
        product = jnp.dot(both, pieces_ref[p], preferred_element_type=F32)
        out_ref[:, p, :] = keep * work_ref[p] + (product[:count] + product[count:])


def per_device(wavefunctions, potential):
    count, depth, plane = wavefunctions.shape
    nz, ny = lax.axis_size("grid"), lax.axis_size("orb") // (2 * NXC)
    scale = 1.0 / (depth * plane * nz)
    vmem = pl.BlockSpec(memory_space=pltpu.VMEM)
    dma = pltpu.SemaphoreType.DMA
    work, pieces, gram, coef = pl.pallas_call(
        functools.partial(gather_kernel, scale),
        out_shape=(
            jax.ShapeDtypeStruct((depth, count, plane), F32),
            jax.ShapeDtypeStruct((depth, 2 * ROWS, plane), BF16),
            jax.ShapeDtypeStruct((ROWS // 2, 2 * ROWS), F32),
            jax.ShapeDtypeStruct((count, 2 * ROWS), F32),
        ),
        in_specs=[vmem, vmem],
        out_specs=(vmem, vmem, vmem, vmem),
        scratch_shapes=[
            pltpu.VMEM((depth, count, plane), F32),
            pltpu.VMEM((2, depth, count, plane), F32),
            pltpu.VMEM((depth, ROWS, plane), F32),
            pltpu.VMEM((ROWS, 2 * ROWS), F32),
            pltpu.VMEM((nz, ROWS // 2, 2 * ROWS), F32),
            pltpu.VMEM((depth, count, plane), F32),
            dma((2, depth)),
            dma((2, depth)),
            dma((9, depth)),
            dma((2 * NXC, depth)),
            dma((nz,)),
            dma((nz,)),
            dma((ny,)),
            dma,
        ],
        compiler_params=pltpu.CompilerParams(collective_id=0, has_side_effects=True),
        name="gather",
    )(wavefunctions, potential)
    return pl.pallas_call(
        correct_kernel,
        out_shape=jax.ShapeDtypeStruct((count, depth, plane), F32),
        in_specs=[vmem] * 4,
        out_specs=vmem,
        scratch_shapes=[pltpu.VMEM((ROWS, 2 * ROWS), F32)],
        name="correct",
    )(work, pieces, gram, coef)


def solution(mesh):
    return jax.shard_map(
        per_device,
        mesh=mesh,
        in_specs=(P("orb", "grid", None), P("grid", None)),
        out_specs=P("orb", "grid", None),
        check_vma=False,
    )
```

```python
import functools

import jax
import jax.numpy as jnp
from jax import lax
from jax.experimental import pallas as pl
from jax.experimental.pallas import tpu as pltpu
from jax.sharding import PartitionSpec as P

PANEL = 32
NPANEL = 2
NY = 32
NXC = 4
ROWS = PANEL * NPANEL

COEFFS = (
    -5369.0 / 1800.0,
    12.0 / 7.0,
    -15.0 / 56.0,
    10.0 / 189.0,
    -1.0 / 112.0,
    2.0 / 1925.0,
    -1.0 / 16632.0,
)
RIM = 6
MESH = pl.DeviceIdType.MESH
LAGS = (3, 6)
F32 = jnp.float32
BF16 = jnp.bfloat16


def split(value):
    high = value.astype(BF16)
    return high, (value - high.astype(F32)).astype(BF16)


def nt(left, right):
    return lax.dot_general(left, right, (((1,), (1,)), ((), ())), preferred_element_type=F32)


def in_plane(v, v0_term):
    width = v.shape[1]
    lane = lax.broadcasted_iota(jnp.int32, v.shape, 1)
    column = lane % NY
    total = v0_term
    for k in range(1, RIM + 1):
        far = k * NY
        part = jnp.where(lane < width - far, pltpu.roll(v, width - far, 1), 0.0)
        part += jnp.where(lane >= far, pltpu.roll(v, far, 1), 0.0)
        part += jnp.where(column < NY - k, pltpu.roll(v, width - k, 1), 0.0)
        part += jnp.where(column >= k, pltpu.roll(v, k, 1), 0.0)
        total += (-0.5 * COEFFS[k]) * part
    return total


def order_of(depth):
    return sorted(range(depth), key=lambda p: (max(depth - p, p + 1), p))


def eliminate(packed):
    row = lax.broadcasted_iota(jnp.int32, (8, 2 * ROWS), 0)
    lane = lax.broadcasted_iota(jnp.int32, (8, 2 * ROWS), 1)
    rolled = pltpu.roll(packed, ROWS, 1)
    tiles, pivots = [], []
    for t in range(ROWS // 8):
        source = rolled if t < ROWS // 16 else packed
        r = (t * 8) % (ROWS // 2)
        tiles.append(jnp.where(lane >= ROWS, source[r : r + 8], jnp.where(lane == row + t * 8, 1.0, 0.0)))
        pivots.append(jnp.ones((8, 2 * ROWS), F32))

    def spread(tile, r):
        return jnp.broadcast_to(tile[r : r + 1, :], tile.shape)

    width = 4
    for k in range(0, ROWS, width):
        b, r = k // 8, k % 8
        below = range(b, ROWS // 8)
        columns = [
            {t: jnp.broadcast_to(tiles[t][:, ROWS + k + j : ROWS + k + j + 1], (8, 2 * ROWS)) for t in below}
            for j in range(width)
        ]
        rows = [spread(tiles[b], r + i) for i in range(width)]
        square = [[spread(columns[j][b], r + i) for j in range(width)] for i in range(width)]
        for i in range(width):
            inverse = 1.0 / square[i][i]
            pivots[b] = jnp.where(row == r + i, square[i][i], pivots[b])
            ratio = {j: square[i][j] * inverse for j in range(i + 1, width)}
            for j in range(i + 1, width):
                for m in range(i + 1, width):
                    square[m][j] = square[m][j] - square[m][i] * ratio[j]
                for t in below:
                    columns[j][t] = columns[j][t] - columns[i][t] * ratio[j]
                rows[j] = rows[j] - ratio[j] * rows[i]
            rows[i] = rows[i] * inverse
        for t in below:
            tile = tiles[t]
            for i in range(width):
                column = columns[i][t]
                if t == b:
                    column = jnp.where(row > r + i, column, 0.0)
                tile = tile - column * rows[i]
            tiles[t] = tile
    return [tile * lax.rsqrt(pivot) for tile, pivot in zip(tiles, pivots)]


def step_kernel(
    scale, v_ref, pot_ref, out_ref,
    own, pot, work, halo, panel, pieces, part, zbuf, gram, coef, inverse, rest,
    lsem, hsend, hrecv, asend, arecv, zsend, zrecv, gsend, grecv, near, far, ready,
):
    depth, count, plane = out_ref.shape
    nz, norb = lax.axis_size("grid"), lax.axis_size("orb")
    ny = norb // (2 * NXC)
    z, o = lax.axis_index("grid"), lax.axis_index("orb")
    y, x, c = o // (2 * NXC), (o // 2) % NXC, o % 2

    def at(yy, xx, cc):
        return (yy * NXC + xx) * 2 + cc

    partner = at(y, x, 1 - c)
    right, left = at(y, (x + 1) % NXC, c), at(y, (x + NXC - 1) % NXC, c)
    y_up, y_down = at((y + 1) % ny, x, c), at((y + ny - 1) % ny, x, c)
    z_up, z_down = (z + 1) % nz, (z + nz - 1) % nz
    order = order_of(depth)

    barrier = pltpu.get_barrier_semaphore()
    for peer in (z_up, z_down):
        pl.semaphore_signal(barrier, inc=1, device_id=(o, peer), device_id_type=MESH)
    for peer in (y_up, y_down, right, left, partner):
        pl.semaphore_signal(barrier, inc=1, device_id=(peer, z), device_id_type=MESH)
    load_v = pltpu.make_async_copy(v_ref, own, lsem.at[0])
    load_pot = pltpu.make_async_copy(pot_ref, pot, lsem.at[1])
    load_v.start()
    load_pot.start()
    pl.semaphore_wait(barrier, 7)

    arrived = {}
    for i in range(depth):
        for side, p, peer in ((0, depth - 1 - i, z_up), (1, i, z_down)):
            copy = pltpu.make_async_remote_copy(
                src_ref=v_ref.at[p],
                dst_ref=halo.at[side, p],
                send_sem=hsend.at[side, p],
                recv_sem=hrecv.at[side, p],
                device_id=(o, peer),
                device_id_type=MESH,
            )
            copy.start()
            arrived[side, p] = copy

    load_v.wait()
    load_pot.wait()

    def flat(p, carry):
        v = own[p]
        rest[p] = in_plane(v, (pot[pl.ds(p, 1), :] - 1.5 * COEFFS[0]) * v)
        return carry

    lax.fori_loop(0, depth, flat, 0)

    def slab(xx, cc):
        return (xx % NXC) * 2 + cc

    mine = slab(x, c)

    def copy_of(kind, s, p, peer):
        rows = pl.ds(pl.multiple_of(s * count, count), count)
        return pltpu.make_async_remote_copy(
            src_ref=panel.at[p, rows, :],
            dst_ref=panel.at[p, rows, :],
            send_sem=asend.at[kind, p],
            recv_sem=arecv.at[s, p],
            device_id=(peer, z),
            device_id_type=MESH,
        )

    goes_up = y <= ny // 2 - 1
    goes_down = (y == 0) | (y >= ny // 2 + 2)

    seen = set()
    for p in order:
        need = [(0, q) for q in range(p, depth)] + [(1, q) for q in range(0, p + 1)]
        for key in need:
            if key not in seen:
                seen.add(key)
                arrived[key].wait_recv()
        total = rest[p]
        for k in range(1, RIM + 1):
            after = own[p + k] if p + k < depth else halo[1, p + k - depth]
            before = own[p - k] if p - k >= 0 else halo[0, p - k + depth]
            total += (-0.5 * COEFFS[k]) * (after + before)
        work[p] = total

        @pl.when(y == 0)
        def _():
            panel[p, pl.ds(pl.multiple_of(mine * count, count), count), :] = total
            copy_of(0, mine, p, y_up).start()
            copy_of(1, mine, p, y_down).start()
            copy_of(2, mine, p, right).start()
            copy_of(3, mine, p, left).start()
            copy_of(5, mine, p, partner).start()

    for d in (2, nz - 2):
        pl.semaphore_signal(near, inc=1, device_id=(o, (z + d) % nz), device_id_type=MESH)

    lag_near, lag_far = LAGS
    for t in range(depth + lag_far):
        if t < depth:
            p = order[t]

            @pl.when(y != 0)
            def _():
                copy_of(0, mine, p, y_up).wait_recv()

                @pl.when(goes_up)
                def _():
                    copy_of(0, mine, p, y_up).start()

                @pl.when(goes_down)
                def _():
                    copy_of(1, mine, p, y_down).start()

                copy_of(2, mine, p, right).start()
                copy_of(3, mine, p, left).start()
                copy_of(5, mine, p, partner).start()
                if t == 0:
                    pl.semaphore_signal(ready, inc=1, device_id=(at(0, x, c), z), device_id_type=MESH)

        i = t - lag_near
        if 0 <= i < depth:
            p = order[i]
            from_left, from_right = slab(x + NXC - 1, c), slab(x + 1, c)
            copy_of(2, from_left, p, right).wait_recv()
            if i % 2 == 0:
                copy_of(4, from_left, p, right).start()
            copy_of(6, from_left, p, partner).start()
            copy_of(3, from_right, p, left).wait_recv()
            if i % 2 == 1:
                copy_of(4, from_right, p, left).start()
            copy_of(7, from_right, p, partner).start()
        i = t - lag_far
        if 0 <= i < depth:
            p = order[i]
            opposite = slab(x + 2, c)
            copy_of(4, opposite, p, right).wait_recv()
            copy_of(8, opposite, p, partner).start()

    pl.semaphore_wait(near, 2)
    for d in (4, nz - 4):
        pl.semaphore_signal(far, inc=1, device_id=(o, (z + d) % nz), device_id_type=MESH)

    part[...] = jnp.zeros_like(part)
    for p in order:
        for xx in range(NXC):
            copy_of(5, slab(xx, 1 - c), p, partner).wait_recv()
        high, low = split(panel[p])
        both = jnp.concatenate([high, low], axis=0)
        pieces[p] = both

        @pl.when(y == 0)
        def _():
            product = nt(both, both)
            part[...] += product[:ROWS] + product[ROWS:]

        @pl.when(y != 0)
        def _():
            own_high, own_low = split(work[p])
            product = nt(jnp.concatenate([own_high, own_low], axis=0), both)
            part[0:count] += product[:count] + product[count:]

    pl.semaphore_wait(far, 2)

    half_rows = ROWS // 2

    def z_copy(origin, to, slot, rows):
        return pltpu.make_async_remote_copy(
            src_ref=zbuf.at[origin, pl.ds(0, rows), :],
            dst_ref=zbuf.at[origin, pl.ds(0, rows), :],
            send_sem=zsend.at[slot],
            recv_sem=zrecv.at[origin],
            device_id=(o, to),
            device_id_type=MESH,
        )

    def z_send(rows):
        for i in range(nz // 2, 0, -1):
            for d in sorted({i, nz - i}):
                z_copy(z, (z + d) % nz, d, rows).start()

    def z_take(rows):
        def take(d, carry):
            z_copy((z + d) % nz, z, 0, rows).wait_recv()
            return carry

        lax.fori_loop(1, nz, take, 0)
        total = zbuf[0, 0:rows]
        for i in range(1, nz):
            total += zbuf[i, 0:rows]
        return total

    def z_done(rows):
        def done(d, carry):
            z_copy(z, (z + d) % nz, d, rows).wait_send()
            return carry

        lax.fori_loop(1, nz, done, 0)

    def g_copy(d):
        return pltpu.make_async_remote_copy(
            src_ref=gram,
            dst_ref=gram,
            send_sem=gsend.at[d],
            recv_sem=grecv,
            device_id=(at((y + d) % ny, x, c), z),
            device_id_type=MESH,
        )

    @pl.when(y == 0)
    def _():
        both = part[...]
        both = (both + pltpu.roll(both, ROWS, 1)) * scale
        lane = lax.broadcasted_iota(jnp.int32, (half_rows, 2 * ROWS), 1)
        zbuf[z] = jnp.where(lane < ROWS, both[:half_rows], both[half_rows:])
        z_send(half_rows)
        pl.semaphore_wait(ready, ny - 1)
        gram[...] = z_take(half_rows)
        for i in range(ny // 2, 0, -1):
            for d in sorted({i, ny - i}):
                g_copy(d).start()

    @pl.when(y != 0)
    def _():
        both = part[0:count]
        zbuf[z, 0:count] = (both + pltpu.roll(both, ROWS, 1)) * scale
        z_send(count)
        g_copy(1).wait_recv()

    tiles = eliminate(gram[...])
    for t, tile in enumerate(tiles):
        inverse[pl.ds(t * 8, 8), :] = tile
    lower_inverse = inverse[:, :ROWS]
    high = lax.Precision.HIGHEST
    solver = lax.dot_general(
        lower_inverse, lower_inverse, (((0,), (0,)), ((), ())), precision=high, preferred_element_type=F32
    )

    @pl.when(y == 0)
    def _():
        coef[...] = inverse[pl.ds(pl.multiple_of(mine * count, count), count), :]

    @pl.when(y != 0)
    def _():
        sums = z_take(count)[:, :ROWS]
        coef[:, :ROWS] = -jnp.dot(sums, solver, precision=high, preferred_element_type=F32)

    f_high, f_low = split(coef[:, :ROWS])
    factor = jnp.concatenate(
        [jnp.concatenate([f_high, f_high], axis=1), jnp.concatenate([f_low, f_low], axis=1)], axis=0
    )
    keep = jnp.where(y == 0, 0.0, 1.0)
    for p in range(depth):
        product = jnp.dot(factor, pieces[p], preferred_element_type=F32)
        out_ref[p] = keep * work[p] + (product[:count] + product[count:])

    for copy in arrived.values():
        copy.wait_send()
    for p in range(depth):

        @pl.when(goes_up)
        def _():
            copy_of(0, mine, p, y_up).wait_send()

        @pl.when(goes_down)
        def _():
            copy_of(1, mine, p, y_down).wait_send()

        for kind in range(2, 9):
            copy_of(kind, mine, p, partner).wait_send()

    @pl.when(y == 0)
    def _():
        z_done(half_rows)
        for d in range(1, ny):
            g_copy(d).wait_send()

    @pl.when(y != 0)
    def _():
        z_done(count)


def per_device(wavefunctions, potential):
    count, depth, plane = wavefunctions.shape
    nz, ny = lax.axis_size("grid"), lax.axis_size("orb") // (2 * NXC)
    scale = 1.0 / (depth * plane * nz)
    dma, plain = pltpu.SemaphoreType.DMA, pltpu.SemaphoreType.REGULAR
    out = pl.pallas_call(
        functools.partial(step_kernel, scale),
        out_shape=jax.ShapeDtypeStruct((depth, count, plane), F32),
        in_specs=[pl.BlockSpec(memory_space=pl.ANY)] * 2,
        out_specs=pl.BlockSpec(memory_space=pltpu.VMEM),
        scratch_shapes=[
            pltpu.VMEM((depth, count, plane), F32),
            pltpu.VMEM((depth, plane), F32),
            pltpu.VMEM((depth, count, plane), F32),
            pltpu.VMEM((2, depth, count, plane), F32),
            pltpu.VMEM((depth, ROWS, plane), F32),
            pltpu.VMEM((depth, 2 * ROWS, plane), BF16),
            pltpu.VMEM((ROWS, 2 * ROWS), F32),
            pltpu.VMEM((nz, ROWS // 2, 2 * ROWS), F32),
            pltpu.VMEM((ROWS // 2, 2 * ROWS), F32),
            pltpu.VMEM((count, 2 * ROWS), F32),
            pltpu.VMEM((ROWS, 2 * ROWS), F32),
            pltpu.VMEM((depth, count, plane), F32),
            dma((2,)),
            dma((2, depth)),
            dma((2, depth)),
            dma((9, depth)),
            dma((2 * NXC, depth)),
            dma((nz,)),
            dma((nz,)),
            dma((ny,)),
            dma,
            plain,
            plain,
            plain,
        ],
        compiler_params=pltpu.CompilerParams(collective_id=0, has_side_effects=True),
        name="step",
    )(jnp.transpose(wavefunctions, (1, 0, 2)), potential)
    return jnp.transpose(out, (1, 0, 2))


def solution(mesh):
    return jax.shard_map(
        per_device,
        mesh=mesh,
        in_specs=(P("orb", "grid", None), P("grid", None)),
        out_specs=P("orb", "grid", None),
        check_vma=False,
    )
```

```python
import functools

import jax
import jax.numpy as jnp
from jax import lax
from jax.experimental import pallas as pl
from jax.experimental.pallas import tpu as pltpu
from jax.sharding import PartitionSpec as P

PANEL = 32
NPANEL = 2
NY = 32
NXC = 4
ROWS = PANEL * NPANEL

COEFFS = (
    -5369.0 / 1800.0,
    12.0 / 7.0,
    -15.0 / 56.0,
    10.0 / 189.0,
    -1.0 / 112.0,
    2.0 / 1925.0,
    -1.0 / 16632.0,
)
RIM = 6
MESH = pl.DeviceIdType.MESH
BLOCK = 128
F32 = jnp.float32
BF16 = jnp.bfloat16


def split(value):
    high = value.astype(BF16)
    return high, (value - high.astype(F32)).astype(BF16)


def nt(left, right):
    return lax.dot_general(left, right, (((1,), (1,)), ((), ())), preferred_element_type=F32)


def in_plane(v, v0_term):
    width = v.shape[1]
    lane = lax.broadcasted_iota(jnp.int32, v.shape, 1)
    column = lane % NY
    total = v0_term
    for k in range(1, RIM + 1):
        far = k * NY
        part = jnp.where(lane < width - far, pltpu.roll(v, width - far, 1), 0.0)
        part += jnp.where(lane >= far, pltpu.roll(v, far, 1), 0.0)
        part += jnp.where(column < NY - k, pltpu.roll(v, width - k, 1), 0.0)
        part += jnp.where(column >= k, pltpu.roll(v, k, 1), 0.0)
        total += (-0.5 * COEFFS[k]) * part
    return total


def eliminate(packed):
    row = lax.broadcasted_iota(jnp.int32, (8, 2 * ROWS), 0)
    lane = lax.broadcasted_iota(jnp.int32, (8, 2 * ROWS), 1)
    rolled = pltpu.roll(packed, ROWS, 1)
    tiles, pivots = [], []
    for t in range(ROWS // 8):
        source = rolled if t < ROWS // 16 else packed
        r = (t * 8) % (ROWS // 2)
        tiles.append(jnp.where(lane >= ROWS, source[r : r + 8], jnp.where(lane == row + t * 8, 1.0, 0.0)))
        pivots.append(jnp.ones((8, 2 * ROWS), F32))

    def spread(tile, r):
        return jnp.broadcast_to(tile[r : r + 1, :], tile.shape)

    width = 4
    for k in range(0, ROWS, width):
        b, r = k // 8, k % 8
        below = range(b, ROWS // 8)
        columns = [
            {t: jnp.broadcast_to(tiles[t][:, ROWS + k + j : ROWS + k + j + 1], (8, 2 * ROWS)) for t in below}
            for j in range(width)
        ]
        rows = [spread(tiles[b], r + i) for i in range(width)]
        square = [[spread(columns[j][b], r + i) for j in range(width)] for i in range(width)]
        for i in range(width):
            inverse = 1.0 / square[i][i]
            pivots[b] = jnp.where(row == r + i, square[i][i], pivots[b])
            ratio = {j: square[i][j] * inverse for j in range(i + 1, width)}
            for j in range(i + 1, width):
                for m in range(i + 1, width):
                    square[m][j] = square[m][j] - square[m][i] * ratio[j]
                for t in below:
                    columns[j][t] = columns[j][t] - columns[i][t] * ratio[j]
                rows[j] = rows[j] - ratio[j] * rows[i]
            rows[i] = rows[i] * inverse
        for t in below:
            tile = tiles[t]
            for i in range(width):
                column = columns[i][t]
                if t == b:
                    column = jnp.where(row > r + i, column, 0.0)
                tile = tile - column * rows[i]
            tiles[t] = tile
    return [tile * lax.rsqrt(pivot) for tile, pivot in zip(tiles, pivots)]


def step_kernel(
    scale, v_ref, pot_ref, out_ref,
    own, pot, work, halo, panel, pieces, part, zbuf, gram, coef, inverse, rest,
    lsem, hsend, hrecv, asend, arecv, zsend, zrecv, gsend, grecv, near, far, ready,
):
    depth, count, plane = out_ref.shape
    nz, norb = lax.axis_size("grid"), lax.axis_size("orb")
    ny = norb // (2 * NXC)
    z, o = lax.axis_index("grid"), lax.axis_index("orb")
    y, x, c = o // (2 * NXC), (o // 2) % NXC, o % 2

    def at(yy, xx, cc):
        return (yy * NXC + xx) * 2 + cc

    partner = at(y, x, 1 - c)
    right, left = at(y, (x + 1) % NXC, c), at(y, (x + NXC - 1) % NXC, c)
    y_up, y_down = at((y + 1) % ny, x, c), at((y + ny - 1) % ny, x, c)
    z_up, z_down = (z + 1) % nz, (z + nz - 1) % nz
    blocks = plane // BLOCK

    def lanes(b):
        return pl.ds(b * BLOCK, BLOCK)

    barrier = pltpu.get_barrier_semaphore()
    for peer in (z_up, z_down):
        pl.semaphore_signal(barrier, inc=1, device_id=(o, peer), device_id_type=MESH)
    for peer in (y_up, y_down, right, left, partner):
        pl.semaphore_signal(barrier, inc=1, device_id=(peer, z), device_id_type=MESH)
    load_v = pltpu.make_async_copy(v_ref, own, lsem.at[0])
    load_pot = pltpu.make_async_copy(pot_ref, pot, lsem.at[1])
    load_v.start()
    load_pot.start()
    pl.semaphore_wait(barrier, 7)

    arrived = {}
    for b in range(blocks):
        for side, peer in ((0, z_up), (1, z_down)):
            copy = pltpu.make_async_remote_copy(
                src_ref=v_ref.at[:, :, lanes(b)],
                dst_ref=halo.at[side, :, :, lanes(b)],
                send_sem=hsend.at[side, b],
                recv_sem=hrecv.at[side, b],
                device_id=(o, peer),
                device_id_type=MESH,
            )
            copy.start()
            arrived[side, b] = copy

    load_v.wait()
    load_pot.wait()

    def flat(p, carry):
        v = own[p]
        rest[p] = in_plane(v, (pot[pl.ds(p, 1), :] - 1.5 * COEFFS[0]) * v)
        return carry

    lax.fori_loop(0, depth, flat, 0)

    def slab(xx, cc):
        return (xx % NXC) * 2 + cc

    mine = slab(x, c)

    def copy_of(kind, s, b, peer):
        piece = panel.at[:, pl.ds(pl.multiple_of(s * count, count), count), lanes(b)]
        return pltpu.make_async_remote_copy(
            src_ref=piece,
            dst_ref=piece,
            send_sem=asend.at[kind, b],
            recv_sem=arecv.at[s, b],
            device_id=(peer, z),
            device_id_type=MESH,
        )

    goes_up = y <= ny // 2 - 1
    goes_down = (y == 0) | (y >= ny // 2 + 2)

    for b in range(blocks):
        for side in range(2):
            arrived[side, b].wait_recv()
        line = [halo[0, p, :, lanes(b)] for p in range(depth)]
        line += [own[p, :, lanes(b)] for p in range(depth)]
        line += [halo[1, p, :, lanes(b)] for p in range(depth)]
        for p in range(depth):
            total = rest[p, :, lanes(b)]
            for k in range(1, RIM + 1):
                total += (-0.5 * COEFFS[k]) * (line[depth + p + k] + line[depth + p - k])
            work[p, :, lanes(b)] = total

        @pl.when(y == 0)
        def _():
            for p in range(depth):
                panel[p, pl.ds(pl.multiple_of(mine * count, count), count), lanes(b)] = work[p, :, lanes(b)]
            copy_of(2, mine, b, right).start()
            copy_of(3, mine, b, left).start()
            copy_of(0, mine, b, y_up).start()
            copy_of(1, mine, b, y_down).start()
            copy_of(5, mine, b, partner).start()

    for d in (2, nz - 2):
        pl.semaphore_signal(near, inc=1, device_id=(o, (z + d) % nz), device_id_type=MESH)

    part[...] = jnp.zeros_like(part)

    def inner_products(pair):
        for b in (pair, pair + 1):
            for xx in range(NXC):
                copy_of(5, slab(xx, 1 - c), b, partner).wait_recv()
        two = pl.ds(pair * BLOCK, 2 * BLOCK)
        for p in range(depth):
            high, low = split(panel[p, :, two])
            pieces[p, :, two] = jnp.concatenate([high, low], axis=0)

        @pl.when(y == 0)
        def _():
            total = jnp.zeros((2 * ROWS, 2 * ROWS), F32)
            for p in range(depth):
                both = pieces[p, :, two]
                total += nt(both, both)
            part[...] += total[:ROWS] + total[ROWS:]

        @pl.when(y != 0)
        def _():
            total = jnp.zeros((2 * count, 2 * ROWS), F32)
            for p in range(depth):
                own_high, own_low = split(work[p, :, two])
                total += nt(jnp.concatenate([own_high, own_low], axis=0), pieces[p, :, two])
            part[0:count] += total[:count] + total[count:]

    at_end = (x == 0) | (x == NXC - 1)
    inside = (x > 0) & (x < NXC - 1)
    relays = [at_end if b < blocks // 2 else inside for b in range(blocks)]

    events = []
    for i in range(blocks):
        events.append((0.55 * i, 0, i))
        events.append((2.6 + 0.8 * i, 1, i))
        events.append((5.0 + 0.8 * i, 2, i))
    from_left, from_right, opposite = slab(x + NXC - 1, c), slab(x + 1, c), slab(x + 2, c)
    for _, what, chunk in sorted(events):
        if what == 0:

            @pl.when(y != 0)
            def _():
                copy_of(0, mine, chunk, y_up).wait_recv()

                @pl.when(goes_up)
                def _():
                    copy_of(0, mine, chunk, y_up).start()

                @pl.when(goes_down)
                def _():
                    copy_of(1, mine, chunk, y_down).start()

                copy_of(2, mine, chunk, right).start()
                copy_of(3, mine, chunk, left).start()
                copy_of(5, mine, chunk, partner).start()
                if chunk == 0:
                    for cc in range(2):
                        pl.semaphore_signal(ready, inc=1, device_id=(at(0, x, cc), z), device_id_type=MESH)

        elif what == 1:
            copy_of(2, from_left, chunk, right).wait_recv()

            @pl.when(relays[chunk])
            def _():
                copy_of(4, from_left, chunk, right).start()

            copy_of(6, from_left, chunk, partner).start()
            copy_of(3, from_right, chunk, left).wait_recv()

            @pl.when(relays[chunk])
            def _():
                copy_of(9, from_right, chunk, left).start()

            copy_of(7, from_right, chunk, partner).start()
        else:
            copy_of(4, opposite, chunk, right).wait_recv()
            copy_of(8, opposite, chunk, partner).start()

    pl.semaphore_wait(near, 2)
    for d in (4, nz - 4):
        pl.semaphore_signal(far, inc=1, device_id=(o, (z + d) % nz), device_id_type=MESH)

    for pair in range(0, blocks, 2):
        inner_products(pair)

    pl.semaphore_wait(far, 2)

    half_rows, quarter = ROWS // 2, ROWS // 4

    def z_copy(origin, to, slot, rows):
        return pltpu.make_async_remote_copy(
            src_ref=zbuf.at[origin, pl.ds(0, rows), :],
            dst_ref=zbuf.at[origin, pl.ds(0, rows), :],
            send_sem=zsend.at[slot],
            recv_sem=zrecv.at[origin],
            device_id=(o, to),
            device_id_type=MESH,
        )

    def z_send(rows):
        for i in range(nz // 2, 0, -1):
            for d in sorted({i, nz - i}):
                z_copy(z, (z + d) % nz, d, rows).start()

    def z_take(rows):
        def take(d, carry):
            z_copy((z + d) % nz, z, 0, rows).wait_recv()
            return carry

        lax.fori_loop(1, nz, take, 0)
        total = zbuf[0, 0:rows]
        for i in range(1, nz):
            total += zbuf[i, 0:rows]
        return total

    def z_done(rows):
        def done(d, carry):
            z_copy(z, (z + d) % nz, d, rows).wait_send()
            return carry

        lax.fori_loop(1, nz, done, 0)

    def g_copy(core, d, cc):
        piece = gram.at[pl.ds(pl.multiple_of(core * quarter, quarter), quarter), :]
        return pltpu.make_async_remote_copy(
            src_ref=piece,
            dst_ref=piece,
            send_sem=gsend.at[2 * d + (1 if cc is c else 0)],
            recv_sem=grecv.at[core],
            device_id=(at((y + d) % ny, x, cc), z),
            device_id_type=MESH,
        )

    g_peers = [(d, cc) for i in range(ny // 2, 0, -1) for d in sorted({i, ny - i}) for cc in (c, 1 - c)]
    g_peers.append((0, 1 - c))

    @pl.when(y == 0)
    def _():
        both = part[...]
        both = (both + pltpu.roll(both, ROWS, 1)) * scale
        lane = lax.broadcasted_iota(jnp.int32, (half_rows, 2 * ROWS), 1)
        part[0:half_rows] = jnp.where(lane < ROWS, both[:half_rows], both[half_rows:])
        zbuf[z] = part[pl.ds(pl.multiple_of(c * quarter, quarter), quarter), :]
        z_send(quarter)
        pl.semaphore_wait(ready, 2 * (ny - 1))
        total = z_take(quarter)
        gram[pl.ds(pl.multiple_of(c * quarter, quarter), quarter), :] = total
        for d, cc in g_peers:
            g_copy(c, d, cc).start()
        g_copy(1 - c, 0, 1 - c).wait_recv()

    @pl.when(y != 0)
    def _():
        both = part[0:count]
        zbuf[z, 0:count] = (both + pltpu.roll(both, ROWS, 1)) * scale
        z_send(count)
        for cc in range(2):
            g_copy(cc, 0, c).wait_recv()

    tiles = eliminate(gram[...])
    for t, tile in enumerate(tiles):
        inverse[pl.ds(t * 8, 8), :] = tile
    lower_inverse = inverse[:, :ROWS]
    high = lax.Precision.HIGHEST
    solver = lax.dot_general(
        lower_inverse, lower_inverse, (((0,), (0,)), ((), ())), precision=high, preferred_element_type=F32
    )

    @pl.when(y == 0)
    def _():
        coef[...] = inverse[pl.ds(pl.multiple_of(mine * count, count), count), :]

    @pl.when(y != 0)
    def _():
        sums = z_take(count)[:, :ROWS]
        coef[:, :ROWS] = -jnp.dot(sums, solver, precision=high, preferred_element_type=F32)

    f_high, f_low = split(coef[:, :ROWS])
    factor = jnp.concatenate(
        [jnp.concatenate([f_high, f_high], axis=1), jnp.concatenate([f_low, f_low], axis=1)], axis=0
    )
    keep = jnp.where(y == 0, 0.0, 1.0)
    for p in range(depth):
        product = jnp.dot(factor, pieces[p], preferred_element_type=F32)
        out_ref[p] = keep * work[p] + (product[:count] + product[count:])

    for copy in arrived.values():
        copy.wait_send()
    for b in range(blocks):

        @pl.when(goes_up)
        def _():
            copy_of(0, mine, b, y_up).wait_send()

        @pl.when(goes_down)
        def _():
            copy_of(1, mine, b, y_down).wait_send()

        for kind in (2, 3, 5, 6, 7, 8):
            copy_of(kind, mine, b, partner).wait_send()

        @pl.when(relays[b])
        def _():
            copy_of(4, mine, b, partner).wait_send()
            copy_of(9, mine, b, partner).wait_send()

    @pl.when(y == 0)
    def _():
        z_done(quarter)
        for d, cc in g_peers:
            g_copy(c, d, cc).wait_send()

    @pl.when(y != 0)
    def _():
        z_done(count)


def store_kernel(value_ref, out_ref, sem):
    copy = pltpu.make_async_copy(value_ref, out_ref, sem)
    copy.start()
    copy.wait()


def per_device(wavefunctions, potential):
    count, depth, plane = wavefunctions.shape
    nz, ny = lax.axis_size("grid"), lax.axis_size("orb") // (2 * NXC)
    scale, blocks = 1.0 / (depth * plane * nz), plane // BLOCK
    dma, plain = pltpu.SemaphoreType.DMA, pltpu.SemaphoreType.REGULAR
    out = pl.pallas_call(
        functools.partial(step_kernel, scale),
        out_shape=jax.ShapeDtypeStruct((depth, count, plane), F32),
        in_specs=[pl.BlockSpec(memory_space=pl.ANY)] * 2,
        out_specs=pl.BlockSpec(memory_space=pltpu.VMEM),
        scratch_shapes=[
            pltpu.VMEM((depth, count, plane), F32),
            pltpu.VMEM((depth, plane), F32),
            pltpu.VMEM((depth, count, plane), F32),
            pltpu.VMEM((2, depth, count, plane), F32),
            pltpu.VMEM((depth, ROWS, plane), F32),
            pltpu.VMEM((depth, 2 * ROWS, plane), BF16),
            pltpu.VMEM((ROWS, 2 * ROWS), F32),
            pltpu.VMEM((nz, ROWS // 4, 2 * ROWS), F32),
            pltpu.VMEM((ROWS // 2, 2 * ROWS), F32),
            pltpu.VMEM((count, 2 * ROWS), F32),
            pltpu.VMEM((ROWS, 2 * ROWS), F32),
            pltpu.VMEM((depth, count, plane), F32),
            dma((2,)),
            dma((2, blocks)),
            dma((2, blocks)),
            dma((10, blocks)),
            dma((2 * NXC, blocks)),
            dma((nz,)),
            dma((nz,)),
            dma((2 * ny,)),
            dma((2,)),
            plain,
            plain,
            plain,
        ],
        compiler_params=pltpu.CompilerParams(collective_id=0, has_side_effects=True, vmem_limit_bytes=8 << 20),
        name="step",
    )(
        pltpu.with_memory_space_constraint(jnp.transpose(wavefunctions, (1, 0, 2)), pltpu.MemorySpace.HBM),
        pltpu.with_memory_space_constraint(potential, pltpu.MemorySpace.HBM),
    )
    out = pl.pallas_call(
        store_kernel,
        out_shape=jax.ShapeDtypeStruct((depth, count, plane), F32),
        in_specs=[pl.BlockSpec(memory_space=pl.ANY)],
        out_specs=pl.BlockSpec(memory_space=pl.ANY),
        scratch_shapes=[pltpu.SemaphoreType.DMA],
        compiler_params=pltpu.CompilerParams(vmem_limit_bytes=1 << 20),
        name="store",
    )(out)
    return jnp.transpose(out, (1, 0, 2))


def solution(mesh):
    return jax.shard_map(
        per_device,
        mesh=mesh,
        in_specs=(P("orb", "grid", None), P("grid", None)),
        out_specs=P("orb", "grid", None),
        check_vma=False,
    )
```

```python
import functools

import jax
import jax.numpy as jnp
from jax import lax
from jax.experimental import pallas as pl
from jax.experimental.pallas import tpu as pltpu
from jax.sharding import PartitionSpec as P

PANEL = 32
NPANEL = 2
NY = 32
NXC = 4
ROWS = PANEL * NPANEL

COEFFS = (
    -5369.0 / 1800.0,
    12.0 / 7.0,
    -15.0 / 56.0,
    10.0 / 189.0,
    -1.0 / 112.0,
    2.0 / 1925.0,
    -1.0 / 16632.0,
)
RIM = 6
MESH = pl.DeviceIdType.MESH
GREET = 6
BLOCK = 128
F32 = jnp.float32
BF16 = jnp.bfloat16


def split(value):
    high = value.astype(BF16)
    return high, (value - high.astype(F32)).astype(BF16)


def nt(left, right):
    return lax.dot_general(left, right, (((1,), (1,)), ((), ())), preferred_element_type=F32)


def in_plane(v, v0_term):
    width = v.shape[1]
    lane = lax.broadcasted_iota(jnp.int32, v.shape, 1)
    column = lane % NY
    total = v0_term
    for k in range(1, RIM + 1):
        far = k * NY
        part = jnp.where(lane < width - far, pltpu.roll(v, width - far, 1), 0.0)
        part += jnp.where(lane >= far, pltpu.roll(v, far, 1), 0.0)
        part += jnp.where(column < NY - k, pltpu.roll(v, width - k, 1), 0.0)
        part += jnp.where(column >= k, pltpu.roll(v, k, 1), 0.0)
        total += (-0.5 * COEFFS[k]) * part
    return total


def eliminate(packed):
    row = lax.broadcasted_iota(jnp.int32, (8, 2 * ROWS), 0)
    lane = lax.broadcasted_iota(jnp.int32, (8, 2 * ROWS), 1)
    rolled = pltpu.roll(packed, ROWS, 1)
    tiles, pivots = [], []
    for t in range(ROWS // 8):
        source = rolled if t < ROWS // 16 else packed
        r = (t * 8) % (ROWS // 2)
        tiles.append(jnp.where(lane >= ROWS, source[r : r + 8], jnp.where(lane == row + t * 8, 1.0, 0.0)))
        pivots.append(jnp.ones((8, 2 * ROWS), F32))

    def spread(tile, r):
        return jnp.broadcast_to(tile[r : r + 1, :], tile.shape)

    width = 4
    for k in range(0, ROWS, width):
        b, r = k // 8, k % 8
        below = range(b, ROWS // 8)
        columns = [
            {t: jnp.broadcast_to(tiles[t][:, ROWS + k + j : ROWS + k + j + 1], (8, 2 * ROWS)) for t in below}
            for j in range(width)
        ]
        rows = [spread(tiles[b], r + i) for i in range(width)]
        square = [[spread(columns[j][b], r + i) for j in range(width)] for i in range(width)]
        for i in range(width):
            inverse = 1.0 / square[i][i]
            pivots[b] = jnp.where(row == r + i, square[i][i], pivots[b])
            ratio = {j: square[i][j] * inverse for j in range(i + 1, width)}
            for j in range(i + 1, width):
                for m in range(i + 1, width):
                    square[m][j] = square[m][j] - square[m][i] * ratio[j]
                for t in below:
                    columns[j][t] = columns[j][t] - columns[i][t] * ratio[j]
                rows[j] = rows[j] - ratio[j] * rows[i]
            rows[i] = rows[i] * inverse
        for t in below:
            tile = tiles[t]
            for i in range(width):
                column = columns[i][t]
                if t == b:
                    column = jnp.where(row > r + i, column, 0.0)
                tile = tile - column * rows[i]
            tiles[t] = tile
    return [tile * lax.rsqrt(pivot) for tile, pivot in zip(tiles, pivots)]


def step_kernel(
    scale, v_ref, pot_ref, out_ref,
    own, pot, work, halo, panel, pieces, part, zbuf, gram, coef, inverse, rest,
    lsem, hsend, hrecv, asend, arecv, zsend, zrecv, gsend, grecv, near, far, ready,
):
    depth, count, plane = out_ref.shape
    nz, norb = lax.axis_size("grid"), lax.axis_size("orb")
    ny = norb // (2 * NXC)
    z, o = lax.axis_index("grid"), lax.axis_index("orb")
    y, x, c = o // (2 * NXC), (o // 2) % NXC, o % 2

    def at(yy, xx, cc):
        return (yy * NXC + xx) * 2 + cc

    partner = at(y, x, 1 - c)
    right, left = at(y, (x + 1) % NXC, c), at(y, (x + NXC - 1) % NXC, c)
    y_up, y_down = at((y + 1) % ny, x, c), at((y + ny - 1) % ny, x, c)
    z_up, z_down = (z + 1) % nz, (z + nz - 1) % nz
    blocks = plane // BLOCK

    def lanes(b):
        return pl.ds(b * BLOCK, BLOCK)

    barrier = pltpu.get_barrier_semaphore()
    for peer in (z_up, z_down):
        pl.semaphore_signal(barrier, inc=1, device_id=(o, peer), device_id_type=MESH)
    for peer in (y_up, y_down, right, left, partner):
        pl.semaphore_signal(barrier, inc=1, device_id=(peer, z), device_id_type=MESH)
    load_v = pltpu.make_async_copy(v_ref, own, lsem.at[0])
    load_pot = pltpu.make_async_copy(pot_ref, pot, lsem.at[1])
    load_v.start()
    load_pot.start()
    pl.semaphore_wait(barrier, 7)

    arrived = {}
    for b in range(blocks):
        for side, peer in ((0, z_up), (1, z_down)):
            copy = pltpu.make_async_remote_copy(
                src_ref=v_ref.at[:, :, lanes(b)],
                dst_ref=halo.at[side, :, :, lanes(b)],
                send_sem=hsend.at[side, b],
                recv_sem=hrecv.at[side, b],
                device_id=(o, peer),
                device_id_type=MESH,
            )
            copy.start()
            arrived[side, b] = copy

    load_v.wait()
    load_pot.wait()

    def flat(p, carry):
        v = own[p]
        rest[p] = in_plane(v, (pot[pl.ds(p, 1), :] - 1.5 * COEFFS[0]) * v)
        return carry

    lax.fori_loop(0, depth, flat, 0)

    def slab(xx, cc):
        return (xx % NXC) * 2 + cc

    mine = slab(x, c)

    def copy_of(kind, s, b, peer):
        piece = panel.at[:, pl.ds(pl.multiple_of(s * count, count), count), lanes(b)]
        return pltpu.make_async_remote_copy(
            src_ref=piece,
            dst_ref=piece,
            send_sem=asend.at[kind, b],
            recv_sem=arecv.at[s, b],
            device_id=(peer, z),
            device_id_type=MESH,
        )

    goes_up = y <= ny // 2 - 1
    goes_down = (y == 0) | (y >= ny // 2 + 2)

    for b in range(blocks):
        for side in range(2):
            arrived[side, b].wait_recv()
        line = [halo[0, p, :, lanes(b)] for p in range(depth)]
        line += [own[p, :, lanes(b)] for p in range(depth)]
        line += [halo[1, p, :, lanes(b)] for p in range(depth)]
        for p in range(depth):
            total = rest[p, :, lanes(b)]
            for k in range(1, RIM + 1):
                total += (-0.5 * COEFFS[k]) * (line[depth + p + k] + line[depth + p - k])
            work[p, :, lanes(b)] = total

        @pl.when(y == 0)
        def _():
            for p in range(depth):
                panel[p, pl.ds(pl.multiple_of(mine * count, count), count), lanes(b)] = work[p, :, lanes(b)]
            copy_of(2, mine, b, right).start()
            copy_of(3, mine, b, left).start()
            copy_of(0, mine, b, y_up).start()
            copy_of(1, mine, b, y_down).start()
            copy_of(5, mine, b, partner).start()

    for d in (2, nz - 2):
        pl.semaphore_signal(near, inc=1, device_id=(o, (z + d) % nz), device_id_type=MESH)

    part[...] = jnp.zeros_like(part)

    def inner_products(pair):
        for b in (pair, pair + 1):
            for xx in range(NXC):
                copy_of(5, slab(xx, 1 - c), b, partner).wait_recv()
        two = pl.ds(pair * BLOCK, 2 * BLOCK)
        for p in range(depth):
            high, low = split(panel[p, :, two])
            pieces[p, :, two] = jnp.concatenate([high, low], axis=0)

        @pl.when(y == 0)
        def _():
            total = jnp.zeros((2 * ROWS, 2 * ROWS), F32)
            for p in range(depth):
                both = pieces[p, :, two]
                total += nt(both, both)
            part[...] += total[:ROWS] + total[ROWS:]

        @pl.when(y != 0)
        def _():
            total = jnp.zeros((2 * count, 2 * ROWS), F32)
            for p in range(depth):
                own_high, own_low = split(work[p, :, two])
                total += nt(jnp.concatenate([own_high, own_low], axis=0), pieces[p, :, two])
            part[0:count] += total[:count] + total[count:]

    at_end = (x == 0) | (x == NXC - 1)
    inside = (x > 0) & (x < NXC - 1)
    relays = [at_end if b < blocks // 2 else inside for b in range(blocks)]

    events = []
    for i in range(blocks):
        events.append((0.55 * i, 0, i))
        events.append((2.6 + 0.8 * i, 1, i))
        events.append((5.0 + 0.8 * i, 2, i))
    from_left, from_right, opposite = slab(x + NXC - 1, c), slab(x + 1, c), slab(x + 2, c)
    for _, what, chunk in sorted(events):
        if what == 0:

            @pl.when(y != 0)
            def _():
                copy_of(0, mine, chunk, y_up).wait_recv()

                @pl.when(goes_up)
                def _():
                    copy_of(0, mine, chunk, y_up).start()

                @pl.when(goes_down)
                def _():
                    copy_of(1, mine, chunk, y_down).start()

                copy_of(2, mine, chunk, right).start()
                copy_of(3, mine, chunk, left).start()
                copy_of(5, mine, chunk, partner).start()
                if chunk == 0:
                    for cc in range(2):
                        pl.semaphore_signal(ready, inc=1, device_id=(at(0, x, cc), z), device_id_type=MESH)

        elif what == 1:
            copy_of(2, from_left, chunk, right).wait_recv()

            @pl.when(relays[chunk])
            def _():
                copy_of(4, from_left, chunk, right).start()

            copy_of(6, from_left, chunk, partner).start()
            copy_of(3, from_right, chunk, left).wait_recv()

            @pl.when(relays[chunk])
            def _():
                copy_of(9, from_right, chunk, left).start()

            copy_of(7, from_right, chunk, partner).start()
            if chunk == GREET:
                pl.semaphore_wait(near, 2)
                for d in (4, nz - 4):
                    pl.semaphore_signal(far, inc=1, device_id=(o, (z + d) % nz), device_id_type=MESH)
        else:
            copy_of(4, opposite, chunk, right).wait_recv()
            copy_of(8, opposite, chunk, partner).start()

    for pair in range(0, blocks, 2):
        inner_products(pair)

    pl.semaphore_wait(far, 2)

    half_rows, quarter = ROWS // 2, ROWS // 4

    def z_copy(origin, to, slot, rows):
        return pltpu.make_async_remote_copy(
            src_ref=zbuf.at[origin, pl.ds(0, rows), :],
            dst_ref=zbuf.at[origin, pl.ds(0, rows), :],
            send_sem=zsend.at[slot],
            recv_sem=zrecv.at[origin],
            device_id=(o, to),
            device_id_type=MESH,
        )

    def z_send(rows):
        for i in range(nz // 2, 0, -1):
            for d in sorted({i, nz - i}):
                z_copy(z, (z + d) % nz, d, rows).start()

    def z_take(rows):
        def take(d, carry):
            z_copy((z + d) % nz, z, 0, rows).wait_recv()
            return carry

        lax.fori_loop(1, nz, take, 0)
        total = zbuf[0, 0:rows]
        for i in range(1, nz):
            total += zbuf[i, 0:rows]
        return total

    def z_done(rows):
        def done(d, carry):
            z_copy(z, (z + d) % nz, d, rows).wait_send()
            return carry

        lax.fori_loop(1, nz, done, 0)

    def g_copy(core, d, cc):
        piece = gram.at[pl.ds(pl.multiple_of(core * quarter, quarter), quarter), :]
        return pltpu.make_async_remote_copy(
            src_ref=piece,
            dst_ref=piece,
            send_sem=gsend.at[2 * d + (1 if cc is c else 0)],
            recv_sem=grecv.at[core],
            device_id=(at((y + d) % ny, x, cc), z),
            device_id_type=MESH,
        )

    g_peers = [(d, cc) for i in range(ny // 2, 0, -1) for d in sorted({i, ny - i}) for cc in (c, 1 - c)]
    g_peers.append((0, 1 - c))

    def all_left():
        for copy in arrived.values():
            copy.wait_send()
        for b in range(blocks):

            @pl.when(goes_up)
            def _():
                copy_of(0, mine, b, y_up).wait_send()

            @pl.when(goes_down)
            def _():
                copy_of(1, mine, b, y_down).wait_send()

            for kind in (2, 3, 5, 6, 7, 8):
                copy_of(kind, mine, b, partner).wait_send()

            @pl.when(relays[b])
            def _():
                copy_of(4, mine, b, partner).wait_send()
                copy_of(9, mine, b, partner).wait_send()

    @pl.when(y == 0)
    def _():
        both = part[...]
        both = (both + pltpu.roll(both, ROWS, 1)) * scale
        lane = lax.broadcasted_iota(jnp.int32, (half_rows, 2 * ROWS), 1)
        part[0:half_rows] = jnp.where(lane < ROWS, both[:half_rows], both[half_rows:])
        zbuf[z] = part[pl.ds(pl.multiple_of(c * quarter, quarter), quarter), :]
        z_send(quarter)
        all_left()
        pl.semaphore_wait(ready, 2 * (ny - 1))
        total = z_take(quarter)
        gram[pl.ds(pl.multiple_of(c * quarter, quarter), quarter), :] = total
        for d, cc in g_peers:
            g_copy(c, d, cc).start()
        g_copy(1 - c, 0, 1 - c).wait_recv()

    @pl.when(y != 0)
    def _():
        both = part[0:count]
        zbuf[z, 0:count] = (both + pltpu.roll(both, ROWS, 1)) * scale
        z_send(count)
        all_left()
        for cc in range(2):
            g_copy(cc, 0, c).wait_recv()

    tiles = eliminate(gram[...])
    for t, tile in enumerate(tiles):
        inverse[pl.ds(t * 8, 8), :] = tile
    lower_inverse = inverse[:, :ROWS]
    high = lax.Precision.HIGHEST
    solver = lax.dot_general(
        lower_inverse, lower_inverse, (((0,), (0,)), ((), ())), precision=high, preferred_element_type=F32
    )

    @pl.when(y == 0)
    def _():
        coef[...] = inverse[pl.ds(pl.multiple_of(mine * count, count), count), :]

    @pl.when(y != 0)
    def _():
        sums = z_take(count)[:, :ROWS]
        coef[:, :ROWS] = -jnp.dot(sums, solver, precision=high, preferred_element_type=F32)

    f_high, f_low = split(coef[:, :ROWS])
    factor = jnp.concatenate(
        [jnp.concatenate([f_high, f_high], axis=1), jnp.concatenate([f_low, f_low], axis=1)], axis=0
    )
    keep = jnp.where(y == 0, 0.0, 1.0)
    for p in range(depth):
        product = jnp.dot(factor, pieces[p], preferred_element_type=F32)
        out_ref[p] = keep * work[p] + (product[:count] + product[count:])

    @pl.when(y == 0)
    def _():
        z_done(quarter)
        for d, cc in g_peers:
            g_copy(c, d, cc).wait_send()

    @pl.when(y != 0)
    def _():
        z_done(count)


def store_kernel(value_ref, out_ref, sem):
    copy = pltpu.make_async_copy(value_ref, out_ref, sem)
    copy.start()
    copy.wait()


def per_device(wavefunctions, potential):
    count, depth, plane = wavefunctions.shape
    nz, ny = lax.axis_size("grid"), lax.axis_size("orb") // (2 * NXC)
    scale, blocks = 1.0 / (depth * plane * nz), plane // BLOCK
    dma, plain = pltpu.SemaphoreType.DMA, pltpu.SemaphoreType.REGULAR
    out = pl.pallas_call(
        functools.partial(step_kernel, scale),
        out_shape=jax.ShapeDtypeStruct((depth, count, plane), F32),
        in_specs=[pl.BlockSpec(memory_space=pl.ANY)] * 2,
        out_specs=pl.BlockSpec(memory_space=pltpu.VMEM),
        scratch_shapes=[
            pltpu.VMEM((depth, count, plane), F32),
            pltpu.VMEM((depth, plane), F32),
            pltpu.VMEM((depth, count, plane), F32),
            pltpu.VMEM((2, depth, count, plane), F32),
            pltpu.VMEM((depth, ROWS, plane), F32),
            pltpu.VMEM((depth, 2 * ROWS, plane), BF16),
            pltpu.VMEM((ROWS, 2 * ROWS), F32),
            pltpu.VMEM((nz, ROWS // 4, 2 * ROWS), F32),
            pltpu.VMEM((ROWS // 2, 2 * ROWS), F32),
            pltpu.VMEM((count, 2 * ROWS), F32),
            pltpu.VMEM((ROWS, 2 * ROWS), F32),
            pltpu.VMEM((depth, count, plane), F32),
            dma((2,)),
            dma((2, blocks)),
            dma((2, blocks)),
            dma((10, blocks)),
            dma((2 * NXC, blocks)),
            dma((nz,)),
            dma((nz,)),
            dma((2 * ny,)),
            dma((2,)),
            plain,
            plain,
            plain,
        ],
        compiler_params=pltpu.CompilerParams(collective_id=0, has_side_effects=True, vmem_limit_bytes=8 << 20),
        name="step",
    )(
        pltpu.with_memory_space_constraint(jnp.transpose(wavefunctions, (1, 0, 2)), pltpu.MemorySpace.HBM),
        pltpu.with_memory_space_constraint(potential, pltpu.MemorySpace.HBM),
    )
    out = pl.pallas_call(
        store_kernel,
        out_shape=jax.ShapeDtypeStruct((depth, count, plane), F32),
        in_specs=[pl.BlockSpec(memory_space=pl.ANY)],
        out_specs=pl.BlockSpec(memory_space=pl.ANY),
        scratch_shapes=[pltpu.SemaphoreType.DMA],
        compiler_params=pltpu.CompilerParams(vmem_limit_bytes=1 << 20),
        name="store",
    )(out)
    return jnp.transpose(out, (1, 0, 2))


def solution(mesh):
    return jax.shard_map(
        per_device,
        mesh=mesh,
        in_specs=(P("orb", "grid", None), P("grid", None)),
        out_specs=P("orb", "grid", None),
        check_vma=False,
    )
```

```python
import functools

import jax
import jax.numpy as jnp
from jax import lax
from jax.experimental import pallas as pl
from jax.experimental.pallas import tpu as pltpu
from jax.sharding import PartitionSpec as P

PANEL = 32
NPANEL = 2
NY = 32
NXC = 4
ROWS = PANEL * NPANEL

COEFFS = (
    -5369.0 / 1800.0,
    12.0 / 7.0,
    -15.0 / 56.0,
    10.0 / 189.0,
    -1.0 / 112.0,
    2.0 / 1925.0,
    -1.0 / 16632.0,
)
RIM = 6
MESH = pl.DeviceIdType.MESH
GREET = 2
BLOCK = 256
F32 = jnp.float32
BF16 = jnp.bfloat16


def split(value):
    high = value.astype(BF16)
    return high, (value - high.astype(F32)).astype(BF16)


def nt(left, right):
    return lax.dot_general(left, right, (((1,), (1,)), ((), ())), preferred_element_type=F32)


def in_plane(v, v0_term):
    width = v.shape[1]
    lane = lax.broadcasted_iota(jnp.int32, v.shape, 1)
    column = lane % NY
    total = v0_term
    for k in range(1, RIM + 1):
        far = k * NY
        part = jnp.where(lane < width - far, pltpu.roll(v, width - far, 1), 0.0)
        part += jnp.where(lane >= far, pltpu.roll(v, far, 1), 0.0)
        part += jnp.where(column < NY - k, pltpu.roll(v, width - k, 1), 0.0)
        part += jnp.where(column >= k, pltpu.roll(v, k, 1), 0.0)
        total += (-0.5 * COEFFS[k]) * part
    return total


def eliminate(packed):
    row = lax.broadcasted_iota(jnp.int32, (8, 2 * ROWS), 0)
    lane = lax.broadcasted_iota(jnp.int32, (8, 2 * ROWS), 1)
    rolled = pltpu.roll(packed, ROWS, 1)
    tiles, pivots = [], []
    for t in range(ROWS // 8):
        source = rolled if t < ROWS // 16 else packed
        r = (t * 8) % (ROWS // 2)
        tiles.append(jnp.where(lane >= ROWS, source[r : r + 8], jnp.where(lane == row + t * 8, 1.0, 0.0)))
        pivots.append(jnp.ones((8, 2 * ROWS), F32))

    def spread(tile, r):
        return jnp.broadcast_to(tile[r : r + 1, :], tile.shape)

    width = 8
    for k in range(0, ROWS, width):
        b, r = k // 8, k % 8
        below = range(b, ROWS // 8)
        columns = [
            {t: jnp.broadcast_to(tiles[t][:, ROWS + k + j : ROWS + k + j + 1], (8, 2 * ROWS)) for t in below}
            for j in range(width)
        ]
        rows = [spread(tiles[b], r + i) for i in range(width)]
        square = [[spread(columns[j][b], r + i) for j in range(width)] for i in range(width)]
        for i in range(width):
            inverse = 1.0 / square[i][i]
            pivots[b] = jnp.where(row == r + i, square[i][i], pivots[b])
            ratio = {j: square[i][j] * inverse for j in range(i + 1, width)}
            for j in range(i + 1, width):
                for m in range(i + 1, width):
                    square[m][j] = square[m][j] - square[m][i] * ratio[j]
                for t in below:
                    columns[j][t] = columns[j][t] - columns[i][t] * ratio[j]
                rows[j] = rows[j] - ratio[j] * rows[i]
            rows[i] = rows[i] * inverse
        for t in below:
            tile = tiles[t]
            for i in range(width):
                column = columns[i][t]
                if t == b:
                    column = jnp.where(row > r + i, column, 0.0)
                tile = tile - column * rows[i]
            tiles[t] = tile
    return [tile * lax.rsqrt(pivot) for tile, pivot in zip(tiles, pivots)]


def step_kernel(
    scale, v_ref, pot_ref, out_ref,
    own, pot, work, halo, panel, pieces, part, zbuf, gram, coef, inverse, rest,
    lsem, hsend, hrecv, asend, arecv, zsend, zrecv, gsend, grecv, near, far, ready,
):
    depth, count, plane = out_ref.shape
    nz, norb = lax.axis_size("grid"), lax.axis_size("orb")
    ny = norb // (2 * NXC)
    z, o = lax.axis_index("grid"), lax.axis_index("orb")
    y, x, c = o // (2 * NXC), (o // 2) % NXC, o % 2

    def at(yy, xx, cc):
        return (yy * NXC + xx) * 2 + cc

    partner = at(y, x, 1 - c)
    right, left = at(y, (x + 1) % NXC, c), at(y, (x + NXC - 1) % NXC, c)
    y_up, y_down = at((y + 1) % ny, x, c), at((y + ny - 1) % ny, x, c)
    z_up, z_down = (z + 1) % nz, (z + nz - 1) % nz
    blocks = plane // BLOCK

    def lanes(b):
        return pl.ds(b * BLOCK, BLOCK)

    barrier = pltpu.get_barrier_semaphore()
    for peer in (z_up, z_down):
        pl.semaphore_signal(barrier, inc=1, device_id=(o, peer), device_id_type=MESH)
    for peer in (y_up, y_down, right, left, partner):
        pl.semaphore_signal(barrier, inc=1, device_id=(peer, z), device_id_type=MESH)
    load_v = pltpu.make_async_copy(v_ref, own, lsem.at[0])
    load_pot = pltpu.make_async_copy(pot_ref, pot, lsem.at[1])
    load_v.start()
    load_pot.start()
    pl.semaphore_wait(barrier, 7)

    arrived = {}
    for b in range(blocks):
        for side, peer in ((0, z_up), (1, z_down)):
            copy = pltpu.make_async_remote_copy(
                src_ref=v_ref.at[:, :, lanes(b)],
                dst_ref=halo.at[side, :, :, lanes(b)],
                send_sem=hsend.at[side, b],
                recv_sem=hrecv.at[side, b],
                device_id=(o, peer),
                device_id_type=MESH,
            )
            copy.start()
            arrived[side, b] = copy

    load_v.wait()
    load_pot.wait()

    def flat(p, carry):
        v = own[p]
        rest[p] = in_plane(v, (pot[pl.ds(p, 1), :] - 1.5 * COEFFS[0]) * v)
        return carry

    lax.fori_loop(0, depth, flat, 0)

    def slab(xx, cc):
        return (xx % NXC) * 2 + cc

    mine = slab(x, c)

    def copy_of(kind, s, b, peer):
        piece = panel.at[:, pl.ds(pl.multiple_of(s * count, count), count), lanes(b)]
        return pltpu.make_async_remote_copy(
            src_ref=piece,
            dst_ref=piece,
            send_sem=asend.at[kind, b],
            recv_sem=arecv.at[s, b],
            device_id=(peer, z),
            device_id_type=MESH,
        )

    goes_up = y <= ny // 2 - 1
    goes_down = (y == 0) | (y >= ny // 2 + 2)

    for b in range(blocks):
        for side in range(2):
            arrived[side, b].wait_recv()
        line = [halo[0, p, :, lanes(b)] for p in range(depth)]
        line += [own[p, :, lanes(b)] for p in range(depth)]
        line += [halo[1, p, :, lanes(b)] for p in range(depth)]
        for p in range(depth):
            total = rest[p, :, lanes(b)]
            for k in range(1, RIM + 1):
                total += (-0.5 * COEFFS[k]) * (line[depth + p + k] + line[depth + p - k])
            work[p, :, lanes(b)] = total

        @pl.when(y == 0)
        def _():
            for p in range(depth):
                panel[p, pl.ds(pl.multiple_of(mine * count, count), count), lanes(b)] = work[p, :, lanes(b)]
            copy_of(2, mine, b, right).start()
            copy_of(3, mine, b, left).start()
            copy_of(0, mine, b, y_up).start()
            copy_of(1, mine, b, y_down).start()
            copy_of(5, mine, b, partner).start()

    for d in (2, nz - 2):
        pl.semaphore_signal(near, inc=1, device_id=(o, (z + d) % nz), device_id_type=MESH)

    part[...] = jnp.zeros_like(part)

    def inner_products(pair):
        for b in (pair, pair + 1):
            for xx in range(NXC):
                copy_of(5, slab(xx, 1 - c), b, partner).wait_recv()
        two = pl.ds(pair * BLOCK, 2 * BLOCK)
        for p in range(depth):
            high, low = split(panel[p, :, two])
            pieces[p, :, two] = jnp.concatenate([high, low], axis=0)

        @pl.when(y == 0)
        def _():
            total = jnp.zeros((2 * ROWS, 2 * ROWS), F32)
            for p in range(depth):
                both = pieces[p, :, two]
                total += nt(both, both)
            part[...] += total[:ROWS] + total[ROWS:]

        @pl.when(y != 0)
        def _():
            total = jnp.zeros((2 * count, 2 * ROWS), F32)
            for p in range(depth):
                own_high, own_low = split(work[p, :, two])
                total += nt(jnp.concatenate([own_high, own_low], axis=0), pieces[p, :, two])
            part[0:count] += total[:count] + total[count:]

    at_end = (x == 0) | (x == NXC - 1)
    inside = (x > 0) & (x < NXC - 1)
    relays = [at_end if b < blocks // 2 else inside for b in range(blocks)]

    events = []
    for i in range(blocks):
        events.append((1.1 * i, 0, i))
        events.append((3.1 + 1.6 * i, 1, i))
        events.append((6.0 + 1.6 * i, 2, i))
    from_left, from_right, opposite = slab(x + NXC - 1, c), slab(x + 1, c), slab(x + 2, c)
    for _, what, chunk in sorted(events):
        if what == 0:

            @pl.when(y != 0)
            def _():
                copy_of(0, mine, chunk, y_up).wait_recv()

                @pl.when(goes_up)
                def _():
                    copy_of(0, mine, chunk, y_up).start()

                @pl.when(goes_down)
                def _():
                    copy_of(1, mine, chunk, y_down).start()

                copy_of(2, mine, chunk, right).start()
                copy_of(3, mine, chunk, left).start()
                copy_of(5, mine, chunk, partner).start()
                if chunk == 0:
                    for cc in range(2):
                        pl.semaphore_signal(ready, inc=1, device_id=(at(0, x, cc), z), device_id_type=MESH)

        elif what == 1:
            copy_of(2, from_left, chunk, right).wait_recv()

            @pl.when(relays[chunk])
            def _():
                copy_of(4, from_left, chunk, right).start()

            copy_of(6, from_left, chunk, partner).start()
            copy_of(3, from_right, chunk, left).wait_recv()

            @pl.when(relays[chunk])
            def _():
                copy_of(9, from_right, chunk, left).start()

            copy_of(7, from_right, chunk, partner).start()
            if chunk == GREET:
                pl.semaphore_wait(near, 2)
                for d in (4, nz - 4):
                    pl.semaphore_signal(far, inc=1, device_id=(o, (z + d) % nz), device_id_type=MESH)
        else:
            copy_of(4, opposite, chunk, right).wait_recv()
            copy_of(8, opposite, chunk, partner).start()

    for pair in range(0, blocks, 2):
        inner_products(pair)

    pl.semaphore_wait(far, 2)

    half_rows, quarter = ROWS // 2, ROWS // 4

    def z_copy(origin, to, slot, rows):
        return pltpu.make_async_remote_copy(
            src_ref=zbuf.at[origin, pl.ds(0, rows), :],
            dst_ref=zbuf.at[origin, pl.ds(0, rows), :],
            send_sem=zsend.at[slot],
            recv_sem=zrecv.at[origin],
            device_id=(o, to),
            device_id_type=MESH,
        )

    def z_send(rows):
        for i in range(nz // 2, 0, -1):
            for d in sorted({i, nz - i}):
                z_copy(z, (z + d) % nz, d, rows).start()

    def z_take(rows):
        def take(d, carry):
            z_copy((z + d) % nz, z, 0, rows).wait_recv()
            return carry

        lax.fori_loop(1, nz, take, 0)
        total = zbuf[0, 0:rows]
        for i in range(1, nz):
            total += zbuf[i, 0:rows]
        return total

    def z_done(rows):
        def done(d, carry):
            z_copy(z, (z + d) % nz, d, rows).wait_send()
            return carry

        lax.fori_loop(1, nz, done, 0)

    def g_copy(core, d, cc):
        piece = gram.at[pl.ds(pl.multiple_of(core * quarter, quarter), quarter), :]
        return pltpu.make_async_remote_copy(
            src_ref=piece,
            dst_ref=piece,
            send_sem=gsend.at[2 * d + (1 if cc is c else 0)],
            recv_sem=grecv.at[core],
            device_id=(at((y + d) % ny, x, cc), z),
            device_id_type=MESH,
        )

    g_peers = [(d, cc) for i in range(ny // 2, 0, -1) for d in sorted({i, ny - i}) for cc in (c, 1 - c)]
    g_peers.append((0, 1 - c))

    def all_left():
        for copy in arrived.values():
            copy.wait_send()
        for b in range(blocks):

            @pl.when(goes_up)
            def _():
                copy_of(0, mine, b, y_up).wait_send()

            @pl.when(goes_down)
            def _():
                copy_of(1, mine, b, y_down).wait_send()

            for kind in (2, 3, 5, 6, 7, 8):
                copy_of(kind, mine, b, partner).wait_send()

            @pl.when(relays[b])
            def _():
                copy_of(4, mine, b, partner).wait_send()
                copy_of(9, mine, b, partner).wait_send()

    @pl.when(y == 0)
    def _():
        both = part[...]
        both = (both + pltpu.roll(both, ROWS, 1)) * scale
        lane = lax.broadcasted_iota(jnp.int32, (half_rows, 2 * ROWS), 1)
        part[0:half_rows] = jnp.where(lane < ROWS, both[:half_rows], both[half_rows:])
        zbuf[z] = part[pl.ds(pl.multiple_of(c * quarter, quarter), quarter), :]
        z_send(quarter)
        all_left()
        pl.semaphore_wait(ready, 2 * (ny - 1))
        total = z_take(quarter)
        gram[pl.ds(pl.multiple_of(c * quarter, quarter), quarter), :] = total
        for d, cc in g_peers:
            g_copy(c, d, cc).start()
        g_copy(1 - c, 0, 1 - c).wait_recv()

    @pl.when(y != 0)
    def _():
        both = part[0:count]
        zbuf[z, 0:count] = (both + pltpu.roll(both, ROWS, 1)) * scale
        z_send(count)
        all_left()
        for cc in range(2):
            g_copy(cc, 0, c).wait_recv()

    tiles = eliminate(gram[...])
    for t, tile in enumerate(tiles):
        inverse[pl.ds(t * 8, 8), :] = tile
    lower_inverse = inverse[:, :ROWS]
    high = lax.Precision.HIGHEST
    solver = lax.dot_general(
        lower_inverse, lower_inverse, (((0,), (0,)), ((), ())), precision=high, preferred_element_type=F32
    )

    @pl.when(y == 0)
    def _():
        coef[...] = inverse[pl.ds(pl.multiple_of(mine * count, count), count), :]

    @pl.when(y != 0)
    def _():
        sums = z_take(count)[:, :ROWS]
        coef[:, :ROWS] = -jnp.dot(sums, solver, precision=high, preferred_element_type=F32)

    f_high, f_low = split(coef[:, :ROWS])
    factor = jnp.concatenate(
        [jnp.concatenate([f_high, f_high], axis=1), jnp.concatenate([f_low, f_low], axis=1)], axis=0
    )
    keep = jnp.where(y == 0, 0.0, 1.0)
    for p in range(depth):
        product = jnp.dot(factor, pieces[p], preferred_element_type=F32)
        out_ref[p] = keep * work[p] + (product[:count] + product[count:])

    @pl.when(y == 0)
    def _():
        z_done(quarter)
        for d, cc in g_peers:
            g_copy(c, d, cc).wait_send()

    @pl.when(y != 0)
    def _():
        z_done(count)


def store_kernel(value_ref, out_ref, sem):
    copy = pltpu.make_async_copy(value_ref, out_ref, sem)
    copy.start()
    copy.wait()


def per_device(wavefunctions, potential):
    count, depth, plane = wavefunctions.shape
    nz, ny = lax.axis_size("grid"), lax.axis_size("orb") // (2 * NXC)
    scale, blocks = 1.0 / (depth * plane * nz), plane // BLOCK
    dma, plain = pltpu.SemaphoreType.DMA, pltpu.SemaphoreType.REGULAR
    out = pl.pallas_call(
        functools.partial(step_kernel, scale),
        out_shape=jax.ShapeDtypeStruct((depth, count, plane), F32),
        in_specs=[pl.BlockSpec(memory_space=pl.ANY)] * 2,
        out_specs=pl.BlockSpec(memory_space=pltpu.VMEM),
        scratch_shapes=[
            pltpu.VMEM((depth, count, plane), F32),
            pltpu.VMEM((depth, plane), F32),
            pltpu.VMEM((depth, count, plane), F32),
            pltpu.VMEM((2, depth, count, plane), F32),
            pltpu.VMEM((depth, ROWS, plane), F32),
            pltpu.VMEM((depth, 2 * ROWS, plane), BF16),
            pltpu.VMEM((ROWS, 2 * ROWS), F32),
            pltpu.VMEM((nz, ROWS // 4, 2 * ROWS), F32),
            pltpu.VMEM((ROWS // 2, 2 * ROWS), F32),
            pltpu.VMEM((count, 2 * ROWS), F32),
            pltpu.VMEM((ROWS, 2 * ROWS), F32),
            pltpu.VMEM((depth, count, plane), F32),
            dma((2,)),
            dma((2, blocks)),
            dma((2, blocks)),
            dma((10, blocks)),
            dma((2 * NXC, blocks)),
            dma((nz,)),
            dma((nz,)),
            dma((2 * ny,)),
            dma((2,)),
            plain,
            plain,
            plain,
        ],
        compiler_params=pltpu.CompilerParams(collective_id=0, has_side_effects=True, vmem_limit_bytes=8 << 20),
        name="step",
    )(
        pltpu.with_memory_space_constraint(jnp.transpose(wavefunctions, (1, 0, 2)), pltpu.MemorySpace.HBM),
        pltpu.with_memory_space_constraint(potential, pltpu.MemorySpace.HBM),
    )
    out = pl.pallas_call(
        store_kernel,
        out_shape=jax.ShapeDtypeStruct((depth, count, plane), F32),
        in_specs=[pl.BlockSpec(memory_space=pl.ANY)],
        out_specs=pl.BlockSpec(memory_space=pl.ANY),
        scratch_shapes=[pltpu.SemaphoreType.DMA],
        compiler_params=pltpu.CompilerParams(vmem_limit_bytes=1 << 20),
        name="store",
    )(out)
    return jnp.transpose(out, (1, 0, 2))


def solution(mesh):
    return jax.shard_map(
        per_device,
        mesh=mesh,
        in_specs=(P("orb", "grid", None), P("grid", None)),
        out_specs=P("orb", "grid", None),
        check_vma=False,
    )
```

```python
import functools

import jax
import jax.numpy as jnp
from jax import lax
from jax.experimental import pallas as pl
from jax.experimental.pallas import tpu as pltpu
from jax.sharding import PartitionSpec as P

PANEL = 32
NPANEL = 2
NY = 32
NXC = 4
ROWS = PANEL * NPANEL

COEFFS = (
    -5369.0 / 1800.0,
    12.0 / 7.0,
    -15.0 / 56.0,
    10.0 / 189.0,
    -1.0 / 112.0,
    2.0 / 1925.0,
    -1.0 / 16632.0,
)
RIM = 6
MESH = pl.DeviceIdType.MESH
GREET = 2
BLOCK = 256
F32 = jnp.float32
BF16 = jnp.bfloat16


def split(value):
    high = value.astype(BF16)
    return high, (value - high.astype(F32)).astype(BF16)


def nt(left, right):
    return lax.dot_general(left, right, (((1,), (1,)), ((), ())), preferred_element_type=F32)


def in_plane(v, v0_term):
    width = v.shape[1]
    lane = lax.broadcasted_iota(jnp.int32, v.shape, 1)
    column = lane % NY
    total = v0_term
    for k in range(1, RIM + 1):
        far = k * NY
        part = jnp.where(lane < width - far, pltpu.roll(v, width - far, 1), 0.0)
        part += jnp.where(lane >= far, pltpu.roll(v, far, 1), 0.0)
        part += jnp.where(column < NY - k, pltpu.roll(v, width - k, 1), 0.0)
        part += jnp.where(column >= k, pltpu.roll(v, k, 1), 0.0)
        total += (-0.5 * COEFFS[k]) * part
    return total


def eliminate(packed):
    row = lax.broadcasted_iota(jnp.int32, (8, 2 * ROWS), 0)
    lane = lax.broadcasted_iota(jnp.int32, (8, 2 * ROWS), 1)
    rolled = pltpu.roll(packed, ROWS, 1)
    tiles, pivots = [], []
    for t in range(ROWS // 8):
        source = rolled if t < ROWS // 16 else packed
        r = (t * 8) % (ROWS // 2)
        tiles.append(jnp.where(lane >= ROWS, source[r : r + 8], jnp.where(lane == row + t * 8, 1.0, 0.0)))
        pivots.append(jnp.ones((8, 2 * ROWS), F32))

    def spread(tile, r):
        return jnp.broadcast_to(tile[r : r + 1, :], tile.shape)

    width = 8
    for k in range(0, ROWS, width):
        b, r = k // 8, k % 8
        below = range(b, ROWS // 8)
        columns = [
            {t: jnp.broadcast_to(tiles[t][:, ROWS + k + j : ROWS + k + j + 1], (8, 2 * ROWS)) for t in below}
            for j in range(width)
        ]
        rows = [spread(tiles[b], r + i) for i in range(width)]
        square = [[spread(columns[j][b], r + i) for j in range(width)] for i in range(width)]
        for i in range(width):
            inverse = 1.0 / square[i][i]
            pivots[b] = jnp.where(row == r + i, square[i][i], pivots[b])
            ratio = {j: square[i][j] * inverse for j in range(i + 1, width)}
            for j in range(i + 1, width):
                for m in range(i + 1, width):
                    square[m][j] = square[m][j] - square[m][i] * ratio[j]
                for t in below:
                    columns[j][t] = columns[j][t] - columns[i][t] * ratio[j]
                rows[j] = rows[j] - ratio[j] * rows[i]
            rows[i] = rows[i] * inverse
        for t in below:
            tile = tiles[t]
            for i in range(width):
                column = columns[i][t]
                if t == b:
                    column = jnp.where(row > r + i, column, 0.0)
                tile = tile - column * rows[i]
            tiles[t] = tile
    return [tile * lax.rsqrt(pivot) for tile, pivot in zip(tiles, pivots)]


def step_kernel(
    scale, v_ref, pot_ref, out_ref,
    own, pot, work, halo, panel, pieces, part, zbuf, gram, coef, inverse, rest,
    lsem, hsend, hrecv, asend, arecv, zsend, zrecv, gsend, grecv, near, far, ready,
):
    depth, count, plane = out_ref.shape
    nz, norb = lax.axis_size("grid"), lax.axis_size("orb")
    ny = norb // (2 * NXC)
    z, o = lax.axis_index("grid"), lax.axis_index("orb")
    y, x, c = o // (2 * NXC), (o // 2) % NXC, o % 2

    def at(yy, xx, cc):
        return (yy * NXC + xx) * 2 + cc

    partner = at(y, x, 1 - c)
    right, left = at(y, (x + 1) % NXC, c), at(y, (x + NXC - 1) % NXC, c)
    y_up, y_down = at((y + 1) % ny, x, c), at((y + ny - 1) % ny, x, c)
    z_up, z_down = (z + 1) % nz, (z + nz - 1) % nz
    blocks = plane // BLOCK

    def lanes(b):
        return pl.ds(b * BLOCK, BLOCK)

    barrier = pltpu.get_barrier_semaphore()
    for peer in (z_up, z_down):
        pl.semaphore_signal(barrier, inc=1, device_id=(o, peer), device_id_type=MESH)
    for peer in (y_up, y_down, right, left, partner):
        pl.semaphore_signal(barrier, inc=1, device_id=(peer, z), device_id_type=MESH)
    load_v = pltpu.make_async_copy(v_ref, own, lsem.at[0])
    load_pot = pltpu.make_async_copy(pot_ref, pot, lsem.at[1])
    load_v.start()
    load_pot.start()
    pl.semaphore_wait(barrier, 7)

    arrived = {}
    for b in range(blocks):
        for side, peer in ((0, z_up), (1, z_down)):
            copy = pltpu.make_async_remote_copy(
                src_ref=v_ref.at[:, :, lanes(b)],
                dst_ref=halo.at[side, :, :, lanes(b)],
                send_sem=hsend.at[side, b],
                recv_sem=hrecv.at[side, b],
                device_id=(o, peer),
                device_id_type=MESH,
            )
            copy.start()
            arrived[side, b] = copy

    load_v.wait()
    load_pot.wait()

    def flat(p, carry):
        v = own[p]
        rest[p] = in_plane(v, (pot[pl.ds(p, 1), :] - 1.5 * COEFFS[0]) * v)
        return carry

    lax.fori_loop(0, depth, flat, 0)

    def slab(xx, cc):
        return (xx % NXC) * 2 + cc

    mine = slab(x, c)

    def copy_of(kind, s, b, peer):
        piece = panel.at[:, pl.ds(pl.multiple_of(s * count, count), count), lanes(b)]
        return pltpu.make_async_remote_copy(
            src_ref=piece,
            dst_ref=piece,
            send_sem=asend.at[kind, b],
            recv_sem=arecv.at[s, b],
            device_id=(peer, z),
            device_id_type=MESH,
        )

    goes_up = y <= ny // 2 - 1
    goes_down = (y == 0) | (y >= ny // 2 + 2)

    for b in range(blocks):
        for side in range(2):
            arrived[side, b].wait_recv()
        line = [halo[0, p, :, lanes(b)] for p in range(depth)]
        line += [own[p, :, lanes(b)] for p in range(depth)]
        line += [halo[1, p, :, lanes(b)] for p in range(depth)]
        for p in range(depth):
            total = rest[p, :, lanes(b)]
            for k in range(1, RIM + 1):
                total += (-0.5 * COEFFS[k]) * (line[depth + p + k] + line[depth + p - k])
            work[p, :, lanes(b)] = total

        @pl.when(y == 0)
        def _():
            for p in range(depth):
                panel[p, pl.ds(pl.multiple_of(mine * count, count), count), lanes(b)] = work[p, :, lanes(b)]
            copy_of(0, mine, b, y_up).start()
            copy_of(1, mine, b, y_down).start()
            copy_of(2, mine, b, right).start()
            copy_of(3, mine, b, left).start()
            copy_of(5, mine, b, partner).start()

    for d in (2, nz - 2):
        pl.semaphore_signal(near, inc=1, device_id=(o, (z + d) % nz), device_id_type=MESH)

    part[...] = jnp.zeros_like(part)

    def inner_products(pair):
        for b in (pair, pair + 1):
            for xx in range(NXC):
                copy_of(5, slab(xx, 1 - c), b, partner).wait_recv()
        two = pl.ds(pair * BLOCK, 2 * BLOCK)
        for p in range(depth):
            high, low = split(panel[p, :, two])
            pieces[p, :, two] = jnp.concatenate([high, low], axis=0)

        @pl.when(y == 0)
        def _():
            total = jnp.zeros((2 * ROWS, 2 * ROWS), F32)
            for p in range(depth):
                both = pieces[p, :, two]
                total += nt(both, both)
            part[...] += total[:ROWS] + total[ROWS:]

        @pl.when(y != 0)
        def _():
            total = jnp.zeros((2 * count, 2 * ROWS), F32)
            for p in range(depth):
                own_high, own_low = split(work[p, :, two])
                total += nt(jnp.concatenate([own_high, own_low], axis=0), pieces[p, :, two])
            part[0:count] += total[:count] + total[count:]

    at_end = (x == 0) | (x == NXC - 1)
    inside = (x > 0) & (x < NXC - 1)
    relays = [at_end if b < blocks // 2 else inside for b in range(blocks)]

    events = []
    for i in range(blocks):
        events.append((1.1 * i, 0, i))
        events.append((3.1 + 1.6 * i, 1, i))
        events.append((6.0 + 1.6 * i, 2, i))
    from_left, from_right, opposite = slab(x + NXC - 1, c), slab(x + 1, c), slab(x + 2, c)
    for _, what, chunk in sorted(events):
        if what == 0:

            @pl.when(y != 0)
            def _():
                copy_of(0, mine, chunk, y_up).wait_recv()

                @pl.when(goes_up)
                def _():
                    copy_of(0, mine, chunk, y_up).start()

                @pl.when(goes_down)
                def _():
                    copy_of(1, mine, chunk, y_down).start()

                copy_of(2, mine, chunk, right).start()
                copy_of(3, mine, chunk, left).start()
                copy_of(5, mine, chunk, partner).start()
                if chunk == 0:
                    for cc in range(2):
                        pl.semaphore_signal(ready, inc=1, device_id=(at(0, x, cc), z), device_id_type=MESH)

        elif what == 1:
            copy_of(2, from_left, chunk, right).wait_recv()

            @pl.when(relays[chunk])
            def _():
                copy_of(4, from_left, chunk, right).start()

            copy_of(6, from_left, chunk, partner).start()
            copy_of(3, from_right, chunk, left).wait_recv()

            @pl.when(relays[chunk])
            def _():
                copy_of(9, from_right, chunk, left).start()

            copy_of(7, from_right, chunk, partner).start()
            if chunk == GREET:
                pl.semaphore_wait(near, 2)
                for d in (4, nz - 4):
                    pl.semaphore_signal(far, inc=1, device_id=(o, (z + d) % nz), device_id_type=MESH)
        else:
            copy_of(4, opposite, chunk, right).wait_recv()
            copy_of(8, opposite, chunk, partner).start()

    for pair in range(0, blocks, 2):
        inner_products(pair)

    pl.semaphore_wait(far, 2)

    half_rows, quarter = ROWS // 2, ROWS // 4

    def z_copy(origin, to, slot, rows):
        return pltpu.make_async_remote_copy(
            src_ref=zbuf.at[origin, pl.ds(0, rows), :],
            dst_ref=zbuf.at[origin, pl.ds(0, rows), :],
            send_sem=zsend.at[slot],
            recv_sem=zrecv.at[origin],
            device_id=(o, to),
            device_id_type=MESH,
        )

    def z_send(rows):
        for i in range(nz // 2, 0, -1):
            for d in sorted({i, nz - i}):
                z_copy(z, (z + d) % nz, d, rows).start()

    def z_take(rows):
        def take(d, carry):
            z_copy((z + d) % nz, z, 0, rows).wait_recv()
            return carry

        lax.fori_loop(1, nz, take, 0)
        total = zbuf[0, 0:rows]
        for i in range(1, nz):
            total += zbuf[i, 0:rows]
        return total

    def z_done(rows):
        def done(d, carry):
            z_copy(z, (z + d) % nz, d, rows).wait_send()
            return carry

        lax.fori_loop(1, nz, done, 0)

    def g_copy(core, d, cc):
        piece = gram.at[pl.ds(pl.multiple_of(core * quarter, quarter), quarter), :]
        return pltpu.make_async_remote_copy(
            src_ref=piece,
            dst_ref=piece,
            send_sem=gsend.at[2 * d + (1 if cc is c else 0)],
            recv_sem=grecv.at[core],
            device_id=(at((y + d) % ny, x, cc), z),
            device_id_type=MESH,
        )

    g_peers = [(d, cc) for i in range(ny // 2, 0, -1) for d in sorted({i, ny - i}) for cc in (c, 1 - c)]
    g_peers.append((0, 1 - c))

    def all_left():
        for copy in arrived.values():
            copy.wait_send()
        for b in range(blocks):

            @pl.when(goes_up)
            def _():
                copy_of(0, mine, b, y_up).wait_send()

            @pl.when(goes_down)
            def _():
                copy_of(1, mine, b, y_down).wait_send()

            for kind in (2, 3, 5, 6, 7, 8):
                copy_of(kind, mine, b, partner).wait_send()

            @pl.when(relays[b])
            def _():
                copy_of(4, mine, b, partner).wait_send()
                copy_of(9, mine, b, partner).wait_send()

    @pl.when(y == 0)
    def _():
        both = part[...]
        both = (both + pltpu.roll(both, ROWS, 1)) * scale
        lane = lax.broadcasted_iota(jnp.int32, (half_rows, 2 * ROWS), 1)
        part[0:half_rows] = jnp.where(lane < ROWS, both[:half_rows], both[half_rows:])
        zbuf[z] = part[pl.ds(pl.multiple_of(c * quarter, quarter), quarter), :]
        z_send(quarter)
        all_left()
        pl.semaphore_wait(ready, 2 * (ny - 1))
        total = z_take(quarter)
        gram[pl.ds(pl.multiple_of(c * quarter, quarter), quarter), :] = total
        for d, cc in g_peers:
            g_copy(c, d, cc).start()
        g_copy(1 - c, 0, 1 - c).wait_recv()

    @pl.when(y != 0)
    def _():
        both = part[0:count]
        zbuf[z, 0:count] = (both + pltpu.roll(both, ROWS, 1)) * scale
        z_send(count)
        all_left()
        for cc in range(2):
            g_copy(cc, 0, c).wait_recv()

    tiles = eliminate(gram[...])
    for t, tile in enumerate(tiles):
        inverse[pl.ds(t * 8, 8), :] = tile
    lower_inverse = inverse[:, :ROWS]
    high = lax.Precision.HIGHEST
    solver = lax.dot_general(
        lower_inverse, lower_inverse, (((0,), (0,)), ((), ())), precision=high, preferred_element_type=F32
    )

    @pl.when(y == 0)
    def _():
        coef[...] = inverse[pl.ds(pl.multiple_of(mine * count, count), count), :]

    @pl.when(y != 0)
    def _():
        sums = z_take(count)[:, :ROWS]
        coef[:, :ROWS] = -jnp.dot(sums, solver, precision=high, preferred_element_type=F32)

    f_high, f_low = split(coef[:, :ROWS])
    factor = jnp.concatenate(
        [jnp.concatenate([f_high, f_high], axis=1), jnp.concatenate([f_low, f_low], axis=1)], axis=0
    )
    keep = jnp.where(y == 0, 0.0, 1.0)
    for p in range(depth):
        product = jnp.dot(factor, pieces[p], preferred_element_type=F32)
        out_ref[p] = keep * work[p] + (product[:count] + product[count:])

    @pl.when(y == 0)
    def _():
        z_done(quarter)
        for d, cc in g_peers:
            g_copy(c, d, cc).wait_send()

    @pl.when(y != 0)
    def _():
        z_done(count)


def store_kernel(value_ref, out_ref, sem):
    copy = pltpu.make_async_copy(value_ref, out_ref, sem)
    copy.start()
    copy.wait()


def per_device(wavefunctions, potential):
    count, depth, plane = wavefunctions.shape
    nz, ny = lax.axis_size("grid"), lax.axis_size("orb") // (2 * NXC)
    scale, blocks = 1.0 / (depth * plane * nz), plane // BLOCK
    dma, plain = pltpu.SemaphoreType.DMA, pltpu.SemaphoreType.REGULAR
    out = pl.pallas_call(
        functools.partial(step_kernel, scale),
        out_shape=jax.ShapeDtypeStruct((depth, count, plane), F32),
        in_specs=[pl.BlockSpec(memory_space=pl.ANY)] * 2,
        out_specs=pl.BlockSpec(memory_space=pltpu.VMEM),
        scratch_shapes=[
            pltpu.VMEM((depth, count, plane), F32),
            pltpu.VMEM((depth, plane), F32),
            pltpu.VMEM((depth, count, plane), F32),
            pltpu.VMEM((2, depth, count, plane), F32),
            pltpu.VMEM((depth, ROWS, plane), F32),
            pltpu.VMEM((depth, 2 * ROWS, plane), BF16),
            pltpu.VMEM((ROWS, 2 * ROWS), F32),
            pltpu.VMEM((nz, ROWS // 4, 2 * ROWS), F32),
            pltpu.VMEM((ROWS // 2, 2 * ROWS), F32),
            pltpu.VMEM((count, 2 * ROWS), F32),
            pltpu.VMEM((ROWS, 2 * ROWS), F32),
            pltpu.VMEM((depth, count, plane), F32),
            dma((2,)),
            dma((2, blocks)),
            dma((2, blocks)),
            dma((10, blocks)),
            dma((2 * NXC, blocks)),
            dma((nz,)),
            dma((nz,)),
            dma((2 * ny,)),
            dma((2,)),
            plain,
            plain,
            plain,
        ],
        compiler_params=pltpu.CompilerParams(collective_id=0, has_side_effects=True, vmem_limit_bytes=8 << 20),
        name="step",
    )(
        pltpu.with_memory_space_constraint(jnp.transpose(wavefunctions, (1, 0, 2)), pltpu.MemorySpace.HBM),
        pltpu.with_memory_space_constraint(potential, pltpu.MemorySpace.HBM),
    )
    out = pl.pallas_call(
        store_kernel,
        out_shape=jax.ShapeDtypeStruct((depth, count, plane), F32),
        in_specs=[pl.BlockSpec(memory_space=pl.ANY)],
        out_specs=pl.BlockSpec(memory_space=pl.ANY),
        scratch_shapes=[pltpu.SemaphoreType.DMA],
        compiler_params=pltpu.CompilerParams(vmem_limit_bytes=1 << 20),
        name="store",
    )(out)
    return jnp.transpose(out, (1, 0, 2))


def solution(mesh):
    return jax.shard_map(
        per_device,
        mesh=mesh,
        in_specs=(P("orb", "grid", None), P("grid", None)),
        out_specs=P("orb", "grid", None),
        check_vma=False,
    )
```
